32 devices in a mesh: lvl: 2 (over core), front: 4 (over z), grid: 4 (over y, x).
Axes of the slice: x: 2, y: 2, z: 4, core: 2. Of those that a mesh axis runs over, the one named last changes fastest.
Arguments:
- child_panel: bfloat16 [4, 2, 4, 2, 128, 512], P('front', None, 'grid', 'lvl'), may hold values from -0.6 to 0.6
- child_blocks: int32 [4], P('front'), may hold values from 6 to 8, as said below
- tile_rows: int32 [2, 4, 4, 64], P('lvl', 'front', 'grid'), may hold values from 0 to 1
- tile_cols: int32 [2, 4, 4, 64], P('lvl', 'front', 'grid'), may hold values from 0 to 7
- tile_parent: int32 [2, 4, 4, 64, 1], P('lvl', 'front', 'grid'), may hold values from 0 to 3; in each aligned block of 64 rows (0 to 63, 64 to 127, ..., all dimensions but the last counted through in order) at most 32 rows name the same one
- tile_place: int32 [2, 4, 4, 64], P('lvl', 'front', 'grid'), may hold values from 0 to 15
- parent_owner: int32 [4], replicated, may hold values from 0 to 3, each once
- parent_front: float32 [4, 2, 4, 2, 128, 2048], P('front', None, 'grid', 'lvl'), may hold values from -1.5 to 151.5, as said below
Outputs:
- factored: float32 [4, 2, 4, 2, 128, 2048], P('front', None, 'grid', 'lvl')
The draws below stay inside these ranges and needn't reach their ends.
Inputs may be any that keep to these rules, and one draw needn't show every extreme that they name: `child_blocks`: some child front has exactly 8 blocks. `tile_parent`: among the 64 tiles of one device at most 32 name the same parent front, and some parent front is named by exactly 32. `parent_owner`: each front index holds exactly one parent. `parent_front`: the diagonal of each parent's first diagonal block lies between 148.5 and 151.5; all other entries lie within -1.5 to 1.5.
All inputs are finite; a program needn't handle non-finite values.
Results may differ from the reference program's by a relative error of at most 0.00053.
Values may be sent and summed in bfloat16 or wider, within the bound.
A program may use at most 64 MiB of HBM per device.

```python
import math
import jax
import jax.numpy as jnp
import numpy as np
from jax import lax

BLOCK = 256
PANEL = 512
CHILD_SPAN = 8
PARENT_SPAN = 8
SLOTS_DEV = 64
HALF_ROWS = 128
CHILD_LOCAL = 2
PARENT_LOCAL = 2
CAPACITY = 32
FRONT_WIDTH = 2048
FRONTS = 4
N_LVL = 2
N_GRID = 4


def draw_child_panel(key, part):
    shape = (FRONTS, CHILD_LOCAL, N_GRID, N_LVL, HALF_ROWS, PANEL)
    noise_key = jax.random.fold_in(key, 31)
    values = 0.1 * jnp.clip(jax.random.normal(noise_key, shape, jnp.float32), -6.0, 6.0)
    return values.astype(jnp.bfloat16)


def draw_child_blocks(key, part):
    sizes = jax.random.randint(jax.random.fold_in(key, 11), (FRONTS,), CHILD_SPAN - 2, CHILD_SPAN + 1)
    widest = jax.random.randint(jax.random.fold_in(key, 12), (), 0, FRONTS)
    offset = jax.random.randint(jax.random.fold_in(key, 13), (), 1, FRONTS)
    narrow = (widest + offset) % FRONTS
    places = jnp.arange(FRONTS)
    sizes = jnp.where(places == narrow, CHILD_SPAN - 2, sizes)
    return jnp.where(places == widest, CHILD_SPAN, sizes).astype(jnp.int32)


def draw_parent_front(key, part):
    shape = (FRONTS, PARENT_LOCAL, N_GRID, N_LVL, HALF_ROWS, FRONT_WIDTH)
    noise_key = jax.random.fold_in(key, 21)
    noise = 0.5 * jnp.clip(jax.random.normal(noise_key, shape, jnp.float32), -3.0, 3.0)
    block_row = lax.broadcasted_iota(jnp.int32, shape, 1)
    grid_row = lax.broadcasted_iota(jnp.int32, shape, 2)
    level_row = lax.broadcasted_iota(jnp.int32, shape, 3)
    inner_row = lax.broadcasted_iota(jnp.int32, shape, 4)
    column = lax.broadcasted_iota(jnp.int32, shape, 5)
    diagonal = (block_row == 0) & (grid_row == 0) & (level_row * HALF_ROWS + inner_row == column)
    return (noise + 150.0 * diagonal.astype(jnp.float32)).astype(jnp.float32)


def plant(values, key, low, largest):
    dims = values.shape
    index_at = [jax.random.randint(jax.random.fold_in(key, axis), (), 0, dims[axis]) for axis in range(len(dims))]
    values = values.at[tuple(index_at)].set(low)
    longest = dims.index(max(dims))
    index_at[longest] = (index_at[longest] + 1) % dims[longest]
    return values.at[tuple(index_at)].set(largest)


def assign_block(own_key, own, number, rows, number_of, top, bound, slope):
    sequence = jax.random.permutation(own_key, number_of)
    packed, ordinary = shares(number_of, rows * top, bound, slope, True), shares(number_of, rows * top, bound, slope, False)
    places = jnp.arange(number_of)

    def named(sizes, offset_by):
        used = int((sizes > 0).sum())
        fixed = max(1, used // 4)
        shifted = fixed + (places - fixed + offset_by * (used - fixed)) % max(1, number_of - fixed)
        return jnp.zeros((number_of,), jnp.int32).at[sequence[jnp.where(places < fixed, places, shifted)]].set(jnp.asarray(sizes, jnp.int32))

    sizes = jnp.where(number % 4 == 0, named(packed, number // 4), named(ordinary, number - number // 4 - 1))
    mixed = jax.random.permutation(jax.random.fold_in(own, 3), number_of)
    source_of, sink = mixed[0:number_of // 2 * 2:2], mixed[1:number_of // 2 * 2:2]
    margin = jnp.minimum(sizes[source_of] - 1, bound - sizes[sink]) // 2
    margin = jnp.where((source_of == sequence[0]) | (sink == sequence[0]) | (sizes[sink] == 0), 0, jnp.maximum(margin, 0))
    shifted = jax.random.randint(jax.random.fold_in(own, 4), (number_of // 2,), 0, 1 << 20) % (margin + 1)
    sizes = sizes.at[source_of].add(-shifted).at[sink].add(shifted)
    members = jnp.searchsorted(jnp.cumsum(sizes), jnp.arange(rows * top), side="right").astype(jnp.int32)
    table = members.reshape(top, rows).T
    table = table[jax.random.permutation(jax.random.fold_in(own, 1), rows)]
    offset_by = jax.random.randint(jax.random.fold_in(own, 2), (rows, 1), 0, top)
    return jnp.take_along_axis(table, (jnp.arange(top)[None, :] + offset_by) % top, axis=1)


def shares(count, total, bound, slope, full):
    weights = [(1 << 20) // math.isqrt(rank ** slope) + 1 for rank in range(1, count + 1)]
    largest = bound if full else min(bound, max(-(-total // count), total * weights[0] // sum(weights)))
    least = 1 if total - largest >= count - 1 else 0
    holding, spare = [largest] + [least] * (count - 1), total - largest - least * (count - 1)
    while spare > 0:
        free = [i for i in range(1, count) if holding[i] < largest] or [i for i in range(1, count) if holding[i] < bound]
        whole, remaining = sum([weights[i] for i in free]), spare
        for i in free:
            addition = min(bound - holding[i], max(1, remaining * weights[i] // whole), spare)
            holding[i] = holding[i] + addition
            spare = spare - addition
    return np.array(holding)


def setup_inputs(seed: int = 0) -> dict:
    streams_of = jax.random.split(jax.random.key(seed), 9)
    child_panel = draw_child_panel(jax.random.fold_in(streams_of[8], 71), 0)
    child_blocks = draw_child_blocks(jax.random.fold_in(streams_of[8], 71), 0)
    tile_rows = plant(jax.random.randint(streams_of[2], (N_LVL, FRONTS, N_GRID, SLOTS_DEV), 0, CHILD_LOCAL), jax.random.fold_in(streams_of[2], 1), 0, CHILD_LOCAL - 1).astype(jnp.int32)
    tile_cols = plant(jax.random.randint(streams_of[3], (N_LVL, FRONTS, N_GRID, SLOTS_DEV), 0, CHILD_SPAN), jax.random.fold_in(streams_of[3], 1), 0, CHILD_SPAN - 1).astype(jnp.int32)
    tile_parent_keys = jax.random.split(jax.random.fold_in(streams_of[4], 1), N_LVL * FRONTS * N_GRID * SLOTS_DEV // SLOTS_DEV)
    tile_parent_turns = jax.random.permutation(jax.random.fold_in(streams_of[4], 3), N_LVL * FRONTS * N_GRID * SLOTS_DEV // SLOTS_DEV)
    tile_parent = jax.vmap(lambda own, number: assign_block(jax.random.fold_in(streams_of[4], 2), own, number, SLOTS_DEV, FRONTS, 1, CAPACITY, 2))(tile_parent_keys, tile_parent_turns).reshape((N_LVL, FRONTS, N_GRID, SLOTS_DEV, 1))
    tile_place = plant(jax.random.randint(streams_of[5], (N_LVL, FRONTS, N_GRID, SLOTS_DEV), 0, PARENT_LOCAL * PARENT_SPAN), jax.random.fold_in(streams_of[5], 1), 0, (PARENT_LOCAL * PARENT_SPAN) - 1).astype(jnp.int32)
    parent_owner = jax.random.permutation(streams_of[6], FRONTS).astype(jnp.int32)
    parent_front = draw_parent_front(jax.random.fold_in(streams_of[8], 71), 0)
    return dict(child_panel=child_panel, child_blocks=child_blocks, tile_rows=tile_rows, tile_cols=tile_cols, tile_parent=tile_parent, tile_place=tile_place, parent_owner=parent_owner, parent_front=parent_front)


def reference(child_panel, child_blocks, tile_rows, tile_cols, tile_parent, tile_place, parent_owner, parent_front):
    full_panel = child_panel.reshape(FRONTS, CHILD_SPAN * BLOCK, PANEL)
    owners = parent_owner[tile_parent[..., 0]]
    level_ids = jnp.broadcast_to(jnp.arange(N_LVL, dtype=jnp.int32).reshape(N_LVL, 1, 1), (N_LVL, N_GRID, SLOTS_DEV))
    grid_ids = jnp.broadcast_to(jnp.arange(N_GRID, dtype=jnp.int32).reshape(1, N_GRID, 1), (N_LVL, N_GRID, SLOTS_DEV))
    initial = parent_front.reshape(FRONTS, PARENT_LOCAL, N_GRID, N_LVL, HALF_ROWS, PARENT_SPAN, BLOCK)

    def add_child(assembled, child_index):
        panel_rows = full_panel[child_index]
        gram_block = (-jnp.dot(panel_rows.astype(jnp.float32), panel_rows.T.astype(jnp.float32), preferred_element_type=jnp.float32)).astype(jnp.bfloat16)
        gram_block = gram_block.reshape(CHILD_SPAN, N_LVL, HALF_ROWS, CHILD_SPAN, BLOCK)
        row_block = tile_rows[:, child_index] * N_GRID + grid_ids
        col_block = tile_cols[:, child_index]
        picked = gram_block[row_block, level_ids, :, col_block, :]
        child_size = child_blocks[child_index]
        live_tile = (row_block < child_size) & (col_block < child_size)
        update_tiles = jnp.where(live_tile[..., None, None], picked, jnp.zeros((), jnp.bfloat16))
        places = tile_place[:, child_index]
        assembled = assembled.at[owners[:, child_index], places // PARENT_SPAN, grid_ids, level_ids, :, places % PARENT_SPAN, :].add(update_tiles.astype(jnp.float32))
        return (assembled, None)
    assembled, _ = lax.scan(add_child, initial, jnp.arange(FRONTS, dtype=jnp.int32))

    def factor(front_part):
        whole_front = front_part.reshape(PARENT_SPAN * BLOCK, FRONT_WIDTH)
        pivot_block = whole_front[:BLOCK, :BLOCK]
        pivot_block = 0.5 * (pivot_block + pivot_block.T)
        lower_factor = jnp.linalg.cholesky(pivot_block)
        panel_rows = lax.linalg.triangular_solve(lower_factor, whole_front[:, :BLOCK], left_side=False, lower=True, transpose_a=True)
        trailing = whole_front[:, BLOCK:] - jnp.dot(panel_rows, panel_rows[BLOCK:].T, precision=lax.Precision.HIGHEST)
        return jnp.concatenate([panel_rows, trailing], axis=1).reshape(PARENT_LOCAL, N_GRID, N_LVL, HALF_ROWS, FRONT_WIDTH)
    return lax.map(factor, assembled.reshape(FRONTS, PARENT_LOCAL, N_GRID, N_LVL, HALF_ROWS, FRONT_WIDTH))
```

```python
import functools

import jax
import jax.numpy as jnp
from jax import lax
from jax.experimental import pallas as pl
from jax.experimental.pallas import tpu as pltpu
from jax.sharding import PartitionSpec as P

BLOCK = 256
NB = 32
SUB = 8
HIGHEST = lax.Precision.HIGHEST
NT = (((1,), (1,)), ((), ()))
TN = (((0,), (0,)), ((), ()))


def eliminate(work):
    n = BLOCK
    row_ids = lax.broadcasted_iota(jnp.int32, (NB, 1), 0)
    for kb in range(n // NB):
        base = kb * NB
        lo, hi = (0, n + n // 2) if base < n // 2 else (n // 2, 2 * n)
        rows = work[base : base + NB, lo:hi]
        for sub in range(NB // SUB):
            first = base - lo + sub * SUB
            cols = [
                jnp.broadcast_to(rows[:, first + i : first + i + 1], (NB, 128))
                for i in range(SUB)
            ]
            for i in range(SUB):
                j = sub * SUB + i
                inv = lax.rsqrt(cols[i][j : j + 1, :])
                below = jnp.where(row_ids > j, cols[i] * inv, 0.0)
                for m in range(i + 1, SUB):
                    cols[m] = cols[m] - below * (cols[m][j : j + 1, :] * inv)
                width = hi - lo
                inv_wide = jnp.concatenate([inv] * (width // 128), axis=1)
                below_wide = jnp.concatenate([below] * (width // 128), axis=1)
                urow = rows[j : j + 1, :] * inv_wide
                rows = jnp.where(row_ids == j, urow, rows - below_wide * urow)
        work[base : base + NB, lo:hi] = rows
        rest = base + NB
        if rest < n:
            left = rows[:, rest // 128 * 128 - lo : n - lo]
            update = lax.dot_general(
                left, rows, TN, precision=HIGHEST, preferred_element_type=jnp.float32
            )
            work[rest:n, lo:hi] = work[rest:n, lo:hi] - update[rest - rest // 128 * 128 :, :]


def factor_tail(acc, pivot, work, panel_ref):
    n = BLOCK
    whole = pivot[...]
    work[:, :n] = 0.5 * (whole + whole.T)
    work[:, n:] = (
        lax.broadcasted_iota(jnp.int32, (n, n), 0) == lax.broadcasted_iota(jnp.int32, (n, n), 1)
    ).astype(jnp.float32)
    eliminate(work)
    local, half = acc.shape[0], acc.shape[1]
    column = acc[:, :, :n].reshape(local * half, n)
    panel = lax.dot_general(
        column, work[:, n:], NT, precision=HIGHEST, preferred_element_type=jnp.float32
    )
    panel_ref[...] = panel.reshape(local, half, n)


def assemble_kernel(
    count_ref, own_list, pivot_list, gathered, own_rows, parent, raw_pivot,
    acc, panel_ref, tiles, pivot_tiles, pivot, work,
):
    fronts, grids, levels, local, half, depth = gathered.shape
    blocks = grids * local

    def gram(step, carry):
        f, g = step // grids, step % grids
        right = gathered[f, g].reshape(levels * local * half, depth)
        left = jnp.concatenate(
            [own_rows[f].reshape(local * half, depth)]
            + [gathered[f, 0].reshape(levels * local * half, depth)],
            axis=0,
        )
        prod = lax.dot_general(left, right, NT, preferred_element_type=jnp.float32)
        prod = (-prod).astype(jnp.bfloat16)
        for r in range(local):
            for s in range(local):
                at = f * (local * blocks) + r * blocks + s * grids + g
                for m in range(levels):
                    lane = (m * local + s) * half
                    tiles[at, :, m * half : (m + 1) * half] = prod[
                        r * half : (r + 1) * half, lane : lane + half
                    ]
                    for lv in range(levels):
                        row = (local + lv * local + r) * half
                        pivot_tiles[lv, at, :, m * half : (m + 1) * half] = prod[
                            row : row + half, lane : lane + half
                        ]
        return carry

    lax.fori_loop(0, fronts * grids, gram, 0)
    pivot[...] = raw_pivot[...]
    for lv in range(levels):

        def add_pivot(k, carry, lv=lv):
            at = pivot_list[lv, k]
            rows = slice(lv * half, (lv + 1) * half)
            pivot[rows, :] = pivot[rows, :] + pivot_tiles[lv, at].astype(jnp.float32)
            return carry

        lax.fori_loop(0, count_ref[1 + lv], add_pivot, 0)
    acc[...] = parent[...]
    width_blocks = parent.shape[2] // BLOCK

    def add_own(k, carry):
        code = own_list[k]
        at, place = code // 256, code % 256
        r = place // width_blocks
        lanes = pl.ds(pl.multiple_of(place % width_blocks * BLOCK, BLOCK), BLOCK)
        acc[r, :, lanes] = acc[r, :, lanes] + tiles[at].astype(jnp.float32)
        return carry

    lax.fori_loop(0, count_ref[0], add_own, 0)
    factor_tail(acc, pivot, work, panel_ref)


def tail_kernel(parent, raw_pivot, panel_ref, work):
    factor_tail(parent, raw_pivot, work, panel_ref)


def schur_kernel(acc, panel, shared, out):
    local, half, width = acc.shape
    grids, levels = shared.shape[0], shared.shape[1]
    rows = panel[...].reshape(local * half, BLOCK)
    out[:, :, :BLOCK] = panel[...]
    for g in range(grids):
        for lv in range(levels):
            for s in range(local):
                if s == 0 and g == 0:
                    continue
                prod = lax.dot_general(
                    rows, shared[g, lv, s], NT, precision=HIGHEST,
                    preferred_element_type=jnp.float32,
                ).reshape(local, half, half)
                lane = (s * grids + g) * BLOCK + lv * half
                out[:, :, lane : lane + half] = acc[:, :, lane : lane + half] - prod


VMEM = pl.BlockSpec(memory_space=pltpu.VMEM)
SMEM = pl.BlockSpec(memory_space=pltpu.SMEM)


def compact(codes, keep):
    size = codes.shape[0]
    position = jnp.cumsum(keep.astype(jnp.int32)) - 1
    match = (position[None, :] == jnp.arange(size, dtype=jnp.int32)[:, None]) & keep[None, :]
    return jnp.sum(jnp.where(match, codes[None, :], 0), axis=1), jnp.sum(keep.astype(jnp.int32))


def owner_of(parents, parent_owner):
    ids = jnp.arange(parent_owner.shape[0], dtype=jnp.int32)
    return jnp.sum(jnp.where(parents[..., None] == ids, parent_owner, 0), axis=-1)


def gather_all(
    child_panel, child_blocks, tile_rows, tile_cols, tile_parent, tile_place, parent_owner, parent_front
):
    levels, grids, fronts = lax.axis_size("lvl"), lax.axis_size("grid"), lax.axis_size("front")
    me_l, me_g, me_f = lax.axis_index("lvl"), lax.axis_index("grid"), lax.axis_index("front")
    local, half, depth = child_panel.shape[1], child_panel.shape[4], child_panel.shape[5]
    rows_in = child_panel.reshape(1, local, half, depth)
    slots = tile_rows.shape[3]
    blocks = local * grids
    row = tile_rows.reshape(slots)
    col = tile_cols.reshape(slots)
    live = (row * grids + me_g < child_blocks[0]) & (col < child_blocks[0])
    to = jnp.where(live, owner_of(tile_parent.reshape(slots), parent_owner), -1)
    meta = jnp.stack([row, col, to, tile_place.reshape(slots)])[None]
    axes = ("front", "grid", "lvl")
    meta = lax.all_gather(meta, axes, axis=0, tiled=True)
    meta = meta.reshape(fronts, grids, levels, 4, slots)
    first = parent_front[0, :1, 0, 0, :, :BLOCK]
    raw_pivot = lax.all_gather(first, ("grid", "lvl"), axis=0, tiled=True)[:levels]
    raw_pivot = raw_pivot.reshape(levels * half, BLOCK)
    gathered = lax.all_gather(rows_in, axes, axis=0, tiled=True)
    gathered = gathered.reshape(fronts, grids, levels, local, half, depth)
    own_rows = lax.dynamic_slice(
        gathered, (0, me_g, me_l, 0, 0, 0), (fronts, 1, 1, local, half, depth)
    ).reshape(fronts, local, half, depth)
    child = jnp.arange(fronts, dtype=jnp.int32)[:, None] * (local * blocks)

    def codes_of(m):
        return child + m[:, 0] * blocks + m[:, 1]

    mine = lax.dynamic_slice(meta, (0, me_g, me_l, 0, 0), (fronts, 1, 1, 4, slots))[:, 0, 0]
    own_list, own_count = compact(
        (codes_of(mine) * 256 + mine[:, 3]).reshape(-1), (mine[:, 2] == me_f).reshape(-1)
    )
    lists, counts = [], [own_count]
    for lv in range(levels):
        m = meta[:, 0, lv]
        found, count = compact(
            codes_of(m).reshape(-1), ((m[:, 2] == me_f) & (m[:, 3] == 0)).reshape(-1)
        )
        lists.append(found)
        counts.append(count)
    parent = parent_front.reshape(parent_front.shape[1], half, parent_front.shape[5])
    return pl.pallas_call(
        assemble_kernel,
        out_shape=(
            jax.ShapeDtypeStruct(parent.shape, jnp.float32),
            jax.ShapeDtypeStruct((parent.shape[0], half, BLOCK), jnp.float32),
        ),
        in_specs=[SMEM, SMEM, SMEM, VMEM, VMEM, VMEM, VMEM],
        out_specs=(VMEM, VMEM),
        scratch_shapes=[
            pltpu.VMEM((fronts * local * blocks, half, BLOCK), jnp.bfloat16),
            pltpu.VMEM((levels, fronts * local * blocks, half, BLOCK), jnp.bfloat16),
            pltpu.VMEM((BLOCK, BLOCK), jnp.float32),
            pltpu.VMEM((BLOCK, 2 * BLOCK), jnp.float32),
        ],
        compiler_params=pltpu.CompilerParams(vmem_limit_bytes=52 * 1024 * 1024),
        name="assemble",
    )(jnp.stack(counts), own_list, jnp.stack(lists), gathered, own_rows, parent, raw_pivot)


def exchange_tiles(
    child_panel, child_blocks, tile_rows, tile_cols, tile_parent, tile_place, parent_owner, parent_front
):
    levels, grids, fronts = lax.axis_size("lvl"), lax.axis_size("grid"), lax.axis_size("front")
    grid_index = lax.axis_index("grid")
    local, half, depth = child_panel.shape[1], child_panel.shape[4], child_panel.shape[5]
    parent_local, width = parent_front.shape[1], parent_front.shape[5]
    slots = tile_rows.shape[3]
    blocks = width // BLOCK
    capacity = 2 * slots // fronts
    own = child_panel.reshape(local * half, depth)
    view = lax.all_gather(
        own.reshape(1, local, half, depth), ("grid", "lvl"), axis=0, tiled=True
    ).reshape(grids, levels, local, half, depth)
    gram = jnp.einsum("ik,glsjk->isglj", own, view, preferred_element_type=jnp.float32)
    gram = (-gram).astype(jnp.bfloat16).reshape(local, half, local * grids, BLOCK)
    gram = gram.transpose(0, 2, 1, 3).reshape(local * local * grids, half, BLOCK)
    row, col = tile_rows.reshape(slots), tile_cols.reshape(slots)
    live = (row * grids + grid_index < child_blocks[0]) & (col < child_blocks[0])
    ids = jnp.arange(fronts, dtype=jnp.int32)
    owners = owner_of(tile_parent.reshape(slots), parent_owner)
    one_hot = (owners[:, None] == ids[None, :]).astype(jnp.int32)
    rank = jnp.sum((jnp.cumsum(one_hot, axis=0) - 1) * one_hot, axis=1)
    index = owners * capacity + rank
    matches = index[None, :] == jnp.arange(fronts * capacity, dtype=jnp.int32)[:, None]
    filled = jnp.any(matches & live[None, :], axis=1)
    source = jnp.sum(jnp.where(matches, (row * local * grids + col)[None, :], 0), axis=1)
    place = jnp.sum(jnp.where(matches, tile_place.reshape(slots)[None, :], 0), axis=1)
    outgoing = jnp.where(filled[:, None, None], gram[source], jnp.zeros((), jnp.bfloat16))
    positions = jnp.where(filled, place, -1)
    incoming = lax.all_to_all(outgoing, "front", split_axis=0, concat_axis=0, tiled=True)
    landed = lax.all_to_all(positions, "front", split_axis=0, concat_axis=0, tiled=True)
    spots = parent_local * blocks
    selector = (landed[:, None] == jnp.arange(spots, dtype=jnp.int32)[None, :]).astype(jnp.bfloat16)
    contrib = jnp.einsum("sk,sij->kij", selector, incoming, preferred_element_type=jnp.float32)
    contrib = contrib.reshape(parent_local, blocks, half, BLOCK).transpose(0, 2, 1, 3)
    assembled = parent_front.reshape(parent_local, half, width) + contrib.reshape(
        parent_local, half, width
    )
    raw = lax.all_gather(assembled[0, :, :BLOCK][None], ("grid", "lvl"), axis=0, tiled=True)
    raw = raw[:levels].reshape(levels * half, BLOCK)
    panel = pl.pallas_call(
        tail_kernel,
        out_shape=jax.ShapeDtypeStruct((parent_local, half, BLOCK), jnp.float32),
        in_specs=[VMEM, VMEM],
        out_specs=VMEM,
        scratch_shapes=[pltpu.VMEM((BLOCK, 2 * BLOCK), jnp.float32)],
        name="factor",
    )(assembled, raw)
    return assembled, panel


def per_device(*args):
    levels, grids, fronts = lax.axis_size("lvl"), lax.axis_size("grid"), lax.axis_size("front")
    parent_front = args[-1]
    assembled, panel = (gather_all if fronts <= 4 else exchange_tiles)(*args)
    shared = lax.all_gather(panel[None], ("grid", "lvl"), axis=0, tiled=True)
    shared = shared.reshape((grids, levels) + panel.shape)
    result = pl.pallas_call(
        schur_kernel,
        out_shape=jax.ShapeDtypeStruct(assembled.shape, jnp.float32),
        in_specs=[VMEM, VMEM, VMEM],
        out_specs=VMEM,
        compiler_params=pltpu.CompilerParams(vmem_limit_bytes=32 * 1024 * 1024),
        name="schur",
    )(assembled, panel, shared)
    return result.reshape(parent_front.shape)


def solution(mesh):
    return jax.shard_map(
        per_device,
        mesh=mesh,
        in_specs=(
            P("front", None, "grid", "lvl", None, None),
            P("front"),
            P("lvl", "front", "grid", None),
            P("lvl", "front", "grid", None),
            P("lvl", "front", "grid", None, None),
            P("lvl", "front", "grid", None),
            P(),
            P("front", None, "grid", "lvl", None, None),
        ),
        out_specs=P("front", None, "grid", "lvl", None, None),
        check_vma=False,
    )
```

```python
import functools

import jax
import jax.numpy as jnp
from jax import lax
from jax.experimental import pallas as pl
from jax.experimental.pallas import tpu as pltpu
from jax.sharding import PartitionSpec as P

BLOCK = 256
NB = 32
SUB = 8
HIGHEST = lax.Precision.HIGHEST
NT = (((1,), (1,)), ((), ()))
TN = (((0,), (0,)), ((), ()))


def eliminate(work):
    n = BLOCK
    row_ids = lax.broadcasted_iota(jnp.int32, (NB, 1), 0)
    for kb in range(n // NB):
        base = kb * NB
        lo, hi = (0, n + n // 2) if base < n // 2 else (n // 2, 2 * n)
        rows = work[base : base + NB, lo:hi]
        for sub in range(NB // SUB):
            first = base - lo + sub * SUB
            cols = [
                jnp.broadcast_to(rows[:, first + i : first + i + 1], (NB, 128))
                for i in range(SUB)
            ]
            for i in range(SUB):
                j = sub * SUB + i
                inv = lax.rsqrt(cols[i][j : j + 1, :])
                below = jnp.where(row_ids > j, cols[i] * inv, 0.0)
                for m in range(i + 1, SUB):
                    cols[m] = cols[m] - below * (cols[m][j : j + 1, :] * inv)
                width = hi - lo
                inv_wide = jnp.concatenate([inv] * (width // 128), axis=1)
                below_wide = jnp.concatenate([below] * (width // 128), axis=1)
                urow = rows[j : j + 1, :] * inv_wide
                rows = jnp.where(row_ids == j, urow, rows - below_wide * urow)
        work[base : base + NB, lo:hi] = rows
        rest = base + NB
        if rest < n:
            left = rows[:, rest // 128 * 128 - lo : n - lo]
            update = lax.dot_general(
                left, rows, TN, precision=HIGHEST, preferred_element_type=jnp.float32
            )
            work[rest:n, lo:hi] = work[rest:n, lo:hi] - update[rest - rest // 128 * 128 :, :]


def factor_tail(acc, pivot, work, panel_ref):
    n = BLOCK
    whole = pivot[...]
    work[:, :n] = 0.5 * (whole + whole.T)
    work[:, n:] = (
        lax.broadcasted_iota(jnp.int32, (n, n), 0) == lax.broadcasted_iota(jnp.int32, (n, n), 1)
    ).astype(jnp.float32)
    eliminate(work)
    local, half = acc.shape[0], acc.shape[1]
    column = acc[:, :, :n].reshape(local * half, n)
    panel = lax.dot_general(
        column, work[:, n:], NT, precision=HIGHEST, preferred_element_type=jnp.float32
    )
    panel_ref[...] = panel.reshape(local, half, n)


def assemble_kernel(
    count_ref, own_list, pivot_list, gathered, own_rows, parent, raw_pivot,
    acc, panel_ref, tiles, pivot_tiles, pivot, work,
):
    fronts, grids, levels, local, half, depth = gathered.shape
    blocks = grids * local

    def gram(step, carry):
        f, g = step // grids, step % grids
        right = gathered[f, g].reshape(levels * local * half, depth)
        left = jnp.concatenate(
            [own_rows[f].reshape(local * half, depth)]
            + [gathered[f, 0].reshape(levels * local * half, depth)],
            axis=0,
        )
        prod = lax.dot_general(left, right, NT, preferred_element_type=jnp.float32)
        prod = (-prod).astype(jnp.bfloat16)
        for r in range(local):
            for s in range(local):
                at = f * (local * blocks) + r * blocks + s * grids + g
                for m in range(levels):
                    lane = (m * local + s) * half
                    tiles[at, :, m * half : (m + 1) * half] = prod[
                        r * half : (r + 1) * half, lane : lane + half
                    ]
                    for lv in range(levels):
                        row = (local + lv * local + r) * half
                        pivot_tiles[lv, at, :, m * half : (m + 1) * half] = prod[
                            row : row + half, lane : lane + half
                        ]
        return carry

    lax.fori_loop(0, fronts * grids, gram, 0)
    pivot[...] = raw_pivot[...]
    for lv in range(levels):

        def add_pivot(k, carry, lv=lv):
            at = pivot_list[lv, k]
            rows = slice(lv * half, (lv + 1) * half)
            pivot[rows, :] = pivot[rows, :] + pivot_tiles[lv, at].astype(jnp.float32)
            return carry

        lax.fori_loop(0, count_ref[1 + lv], add_pivot, 0)
    acc[...] = parent[...]
    width_blocks = parent.shape[2] // BLOCK

    def add_own(k, carry):
        code = own_list[k]
        at, place = code // 256, code % 256
        r = place // width_blocks
        lanes = pl.ds(pl.multiple_of(place % width_blocks * BLOCK, BLOCK), BLOCK)
        acc[r, :, lanes] = acc[r, :, lanes] + tiles[at].astype(jnp.float32)
        return carry

    lax.fori_loop(0, count_ref[0], add_own, 0)
    factor_tail(acc, pivot, work, panel_ref)


def tail_kernel(parent, raw_pivot, panel_ref, work):
    factor_tail(parent, raw_pivot, work, panel_ref)


def schur_kernel(acc, panel, shared, out):
    local, half, width = acc.shape
    grids, levels = shared.shape[0], shared.shape[1]
    rows = panel[...].reshape(local * half, BLOCK)
    out[:, :, :BLOCK] = panel[...]
    for g in range(grids):
        for lv in range(levels):
            for s in range(local):
                if s == 0 and g == 0:
                    continue
                prod = lax.dot_general(
                    rows, shared[g, lv, s], NT, precision=HIGHEST,
                    preferred_element_type=jnp.float32,
                ).reshape(local, half, half)
                lane = (s * grids + g) * BLOCK + lv * half
                out[:, :, lane : lane + half] = acc[:, :, lane : lane + half] - prod


class Sends:
    def __init__(self, send_sems, recv_sems):
        self.send_sems, self.recv_sems, self.used, self.started = send_sems, recv_sems, 0, []

    def make(self, src, dst, device):
        copy = pltpu.make_async_remote_copy(
            src_ref=src,
            dst_ref=dst,
            send_sem=self.send_sems.at[self.used],
            recv_sem=self.recv_sems.at[self.used],
            device_id=device,
            device_id_type=pl.DeviceIdType.MESH,
        )
        self.used += 1
        return copy

    def start(self, src, dst, device):
        copy = self.make(src, dst, device)
        copy.start()
        self.started.append(copy)
        return copy

    def finish(self):
        for copy in self.started:
            copy.wait_send()


def greet(devices):
    barrier = pltpu.get_barrier_semaphore()
    for device in devices:
        pl.semaphore_signal(barrier, inc=1, device_id=device, device_id_type=pl.DeviceIdType.MESH)
    pl.semaphore_wait(barrier, len(devices))


def plane_peers():
    level, grid = lax.axis_index("lvl"), lax.axis_index("grid")
    across = grid + 1 - 2 * (grid % 2)
    along = (grid + 2) % 4
    return level, grid, across, along


def gather_kernel(
    own, meta, first, out, meta_own, meta_pivot, raw, send_sems, recv_sems, local_sems
):
    level, grid, across, along = plane_peers()
    corner = (across + 2) % 4
    front = lax.axis_index("front")
    order = [front + 1 - 2 * (front % 2), (front + 2) % 4, 3 - front]

    def at_front(f):
        return {"front": f}

    x_peer, y_peer, core = {"grid": across}, {"grid": along}, {"lvl": 1 - level}
    greet([at_front(f) for f in order] + [x_peer, y_peer, {"grid": corner}, core])
    sends = Sends(send_sems, recv_sems)
    locals_ = [
        pltpu.make_async_copy(own, out.at[front, grid, level], local_sems.at[0]),
        pltpu.make_async_copy(meta, meta_own.at[front], local_sems.at[1]),
    ]
    for copy in locals_:
        copy.start()
    meta_z = [sends.start(meta, meta_own.at[front], at_front(f)) for f in order]
    panel_z = [sends.start(own, out.at[front, grid, level], at_front(f)) for f in order]
    to_x, to_y, to_core = [], [], []

    def spread(f, source):
        place = out.at[f, grid, level]
        to_x.append(sends.start(source, place, x_peer))
        to_y.append(sends.start(source, place, y_peer))
        to_core.append(sends.start(source, place, core))

    spread(front, own)
    planes = [front] + order

    raw_at = raw.at[level]
    piv_at = meta_pivot.at[level]
    raw_copies = [sends.make(first, raw_at, {"grid": g}) for g in (1, 2, 3)]
    piv_copies = [sends.make(meta_own, piv_at, {"grid": g}) for g in (1, 2, 3)]
    raw_local = pltpu.make_async_copy(first, raw_at, local_sems.at[2])
    piv_local = pltpu.make_async_copy(meta_own, piv_at, local_sems.at[3])

    locals_[1].wait()
    for copy in meta_z:
        copy.wait_recv()

    @pl.when(grid == 0)
    def _():
        piv_local.start()
        raw_local.start()
        for copy in piv_copies + raw_copies:
            copy.start()
        piv_local.wait()
        raw_local.wait()

    for g in (1, 2, 3):

        @pl.when(grid == g)
        def _(g=g):
            piv_copies[g - 1].wait_recv()
            raw_copies[g - 1].wait_recv()

    small = [sends.start(piv_at, piv_at, core), sends.start(raw_at, raw_at, core)]
    corners = []

    def forward(k):
        f = planes[k]
        to_x[k].wait_recv()
        place = out.at[f, across, level]
        half = out.at[f, across, level, 0]
        corners.append(sends.start(half, half, y_peer))
        to_core.append(sends.start(place, place, core))
        to_y[k].wait_recv()
        place = out.at[f, along, level]
        half = out.at[f, along, level, 1]
        corners.append(sends.start(half, half, x_peer))
        to_core.append(sends.start(place, place, core))

    def corner_in(k):
        place = out.at[planes[k], corner, level]
        corners[2 * k].wait_recv()
        corners[2 * k + 1].wait_recv()
        to_core.append(sends.start(place, place, core))

    for k in (1, 2, 3):
        panel_z[k - 1].wait_recv()
        place = out.at[planes[k], grid, level]
        spread(planes[k], place)
        forward(k - 1)
        if k > 1:
            corner_in(k - 2)
    forward(3)
    corner_in(2)
    corner_in(3)
    locals_[0].wait()
    for copy in to_core + small:
        copy.wait_recv()
    sends.finish()

    @pl.when(grid == 0)
    def _():
        for copy in piv_copies + raw_copies:
            copy.wait_send()


def share_kernel(own, out, send_sems, recv_sems, local_sem):
    level, grid, across, along = plane_peers()
    corner = (across + 2) % 4
    x_peer, y_peer, core = {"grid": across}, {"grid": along}, {"lvl": 1 - level}
    greet([x_peer, y_peer, core])
    sends = Sends(send_sems, recv_sems)
    local = out.shape[2]
    mine = pltpu.make_async_copy(own, out.at[grid, level], local_sem)
    to_x = [None] * local
    to_y = [None] * local
    to_core = []
    for r in range(local):
        place = out.at[grid, level, r]
        to_x[r] = sends.start(own.at[r], place, x_peer)
        place = out.at[grid, level, local - 1 - r]
        to_y[local - 1 - r] = sends.start(own.at[local - 1 - r], place, y_peer)
    to_core.append(sends.start(own, out.at[grid, level], core))
    mine.start()
    to_x[0].wait_recv()
    half = out.at[across, level, 0]
    corner_y = sends.start(half, half, y_peer)
    to_y[1].wait_recv()
    half = out.at[along, level, 1]
    corner_x = sends.start(half, half, x_peer)
    for r in range(1, local):
        to_x[r].wait_recv()
    place = out.at[across, level]
    to_core.append(sends.start(place, place, core))
    to_y[0].wait_recv()
    place = out.at[along, level]
    to_core.append(sends.start(place, place, core))
    corner_y.wait_recv()
    half = out.at[corner, level, 0]
    to_core.append(sends.start(half, half, core))
    corner_x.wait_recv()
    half = out.at[corner, level, 1]
    to_core.append(sends.start(half, half, core))
    mine.wait()
    for copy in to_core:
        copy.wait_recv()
    sends.finish()


VMEM = pl.BlockSpec(memory_space=pltpu.VMEM)
ANY = pl.BlockSpec(memory_space=pl.ANY)
SMEM = pl.BlockSpec(memory_space=pltpu.SMEM)


def compact(codes, keep):
    size = codes.shape[0]
    position = jnp.cumsum(keep.astype(jnp.int32)) - 1
    match = (position[None, :] == jnp.arange(size, dtype=jnp.int32)[:, None]) & keep[None, :]
    return jnp.sum(jnp.where(match, codes[None, :], 0), axis=1), jnp.sum(keep.astype(jnp.int32))


def owner_of(parents, parent_owner):
    ids = jnp.arange(parent_owner.shape[0], dtype=jnp.int32)
    return jnp.sum(jnp.where(parents[..., None] == ids, parent_owner, 0), axis=-1)


def gather_all(
    child_panel, child_blocks, tile_rows, tile_cols, tile_parent, tile_place, parent_owner, parent_front
):
    levels, grids, fronts = lax.axis_size("lvl"), lax.axis_size("grid"), lax.axis_size("front")
    me_l, me_g, me_f = lax.axis_index("lvl"), lax.axis_index("grid"), lax.axis_index("front")
    local, half, depth = child_panel.shape[1], child_panel.shape[4], child_panel.shape[5]
    rows_in = child_panel.reshape(1, local, half, depth)
    slots = tile_rows.shape[3]
    blocks = local * grids
    row = tile_rows.reshape(slots)
    col = tile_cols.reshape(slots)
    live = (row * grids + me_g < child_blocks[0]) & (col < child_blocks[0])
    to = jnp.where(live, owner_of(tile_parent.reshape(slots), parent_owner), -1)
    meta = jnp.stack([row, col, to, tile_place.reshape(slots)])
    gathered, meta_own, meta_pivot, raw_pivot = pl.pallas_call(
        gather_kernel,
        out_shape=(
            jax.ShapeDtypeStruct((fronts, grids, levels, local, half, depth), jnp.bfloat16),
            jax.ShapeDtypeStruct((fronts, 4, slots), jnp.int32),
            jax.ShapeDtypeStruct((levels, fronts, 4, slots), jnp.int32),
            jax.ShapeDtypeStruct((levels, half, BLOCK), jnp.float32),
        ),
        in_specs=[VMEM, VMEM, VMEM],
        out_specs=(VMEM, VMEM, VMEM, VMEM),
        scratch_shapes=[
            pltpu.SemaphoreType.DMA((64,)),
            pltpu.SemaphoreType.DMA((64,)),
            pltpu.SemaphoreType.DMA((4,)),
        ],
        compiler_params=pltpu.CompilerParams(
            collective_id=0, has_side_effects=True, vmem_limit_bytes=24 * 1024 * 1024
        ),
        name="gather",
    )(rows_in[0], meta, parent_front[0, 0, 0, 0, :, :BLOCK])
    raw_pivot = raw_pivot.reshape(levels * half, BLOCK)
    own_rows = lax.dynamic_slice(
        gathered, (0, me_g, me_l, 0, 0, 0), (fronts, 1, 1, local, half, depth)
    ).reshape(fronts, local, half, depth)
    child = jnp.arange(fronts, dtype=jnp.int32)[:, None] * (local * blocks)

    def codes_of(m):
        return child + m[:, 0] * blocks + m[:, 1]

    mine = meta_own
    own_list, own_count = compact(
        (codes_of(mine) * 256 + mine[:, 3]).reshape(-1), (mine[:, 2] == me_f).reshape(-1)
    )
    lists, counts = [], [own_count]
    for lv in range(levels):
        m = meta_pivot[lv]
        found, count = compact(
            codes_of(m).reshape(-1), ((m[:, 2] == me_f) & (m[:, 3] == 0)).reshape(-1)
        )
        lists.append(found)
        counts.append(count)
    parent = parent_front.reshape(parent_front.shape[1], half, parent_front.shape[5])
    return pl.pallas_call(
        assemble_kernel,
        out_shape=(
            jax.ShapeDtypeStruct(parent.shape, jnp.float32),
            jax.ShapeDtypeStruct((parent.shape[0], half, BLOCK), jnp.float32),
        ),
        in_specs=[SMEM, SMEM, SMEM, VMEM, VMEM, VMEM, VMEM],
        out_specs=(VMEM, VMEM),
        scratch_shapes=[
            pltpu.VMEM((fronts * local * blocks, half, BLOCK), jnp.bfloat16),
            pltpu.VMEM((levels, fronts * local * blocks, half, BLOCK), jnp.bfloat16),
            pltpu.VMEM((BLOCK, BLOCK), jnp.float32),
            pltpu.VMEM((BLOCK, 2 * BLOCK), jnp.float32),
        ],
        compiler_params=pltpu.CompilerParams(vmem_limit_bytes=52 * 1024 * 1024),
        name="assemble",
    )(jnp.stack(counts), own_list, jnp.stack(lists), gathered, own_rows, parent, raw_pivot)


def exchange_tiles(
    child_panel, child_blocks, tile_rows, tile_cols, tile_parent, tile_place, parent_owner, parent_front
):
    levels, grids, fronts = lax.axis_size("lvl"), lax.axis_size("grid"), lax.axis_size("front")
    grid_index = lax.axis_index("grid")
    local, half, depth = child_panel.shape[1], child_panel.shape[4], child_panel.shape[5]
    parent_local, width = parent_front.shape[1], parent_front.shape[5]
    slots = tile_rows.shape[3]
    blocks = width // BLOCK
    capacity = 2 * slots // fronts
    own = child_panel.reshape(local * half, depth)
    view = lax.all_gather(
        own.reshape(1, local, half, depth), ("grid", "lvl"), axis=0, tiled=True
    ).reshape(grids, levels, local, half, depth)
    gram = jnp.einsum("ik,glsjk->isglj", own, view, preferred_element_type=jnp.float32)
    gram = (-gram).astype(jnp.bfloat16).reshape(local, half, local * grids, BLOCK)
    gram = gram.transpose(0, 2, 1, 3).reshape(local * local * grids, half, BLOCK)
    row, col = tile_rows.reshape(slots), tile_cols.reshape(slots)
    live = (row * grids + grid_index < child_blocks[0]) & (col < child_blocks[0])
    ids = jnp.arange(fronts, dtype=jnp.int32)
    owners = owner_of(tile_parent.reshape(slots), parent_owner)
    one_hot = (owners[:, None] == ids[None, :]).astype(jnp.int32)
    rank = jnp.sum((jnp.cumsum(one_hot, axis=0) - 1) * one_hot, axis=1)
    index = owners * capacity + rank
    matches = index[None, :] == jnp.arange(fronts * capacity, dtype=jnp.int32)[:, None]
    filled = jnp.any(matches & live[None, :], axis=1)
    source = jnp.sum(jnp.where(matches, (row * local * grids + col)[None, :], 0), axis=1)
    place = jnp.sum(jnp.where(matches, tile_place.reshape(slots)[None, :], 0), axis=1)
    outgoing = jnp.where(filled[:, None, None], gram[source], jnp.zeros((), jnp.bfloat16))
    positions = jnp.where(filled, place, -1)
    incoming = lax.all_to_all(outgoing, "front", split_axis=0, concat_axis=0, tiled=True)
    landed = lax.all_to_all(positions, "front", split_axis=0, concat_axis=0, tiled=True)
    spots = parent_local * blocks
    selector = (landed[:, None] == jnp.arange(spots, dtype=jnp.int32)[None, :]).astype(jnp.bfloat16)
    contrib = jnp.einsum("sk,sij->kij", selector, incoming, preferred_element_type=jnp.float32)
    contrib = contrib.reshape(parent_local, blocks, half, BLOCK).transpose(0, 2, 1, 3)
    assembled = parent_front.reshape(parent_local, half, width) + contrib.reshape(
        parent_local, half, width
    )
    raw = lax.all_gather(assembled[0, :, :BLOCK][None], ("grid", "lvl"), axis=0, tiled=True)
    raw = raw[:levels].reshape(levels * half, BLOCK)
    panel = pl.pallas_call(
        tail_kernel,
        out_shape=jax.ShapeDtypeStruct((parent_local, half, BLOCK), jnp.float32),
        in_specs=[VMEM, VMEM],
        out_specs=VMEM,
        scratch_shapes=[pltpu.VMEM((BLOCK, 2 * BLOCK), jnp.float32)],
        name="factor",
    )(assembled, raw)
    return assembled, panel


def per_device(*args):
    levels, grids, fronts = lax.axis_size("lvl"), lax.axis_size("grid"), lax.axis_size("front")
    parent_front = args[-1]
    assembled, panel = (gather_all if fronts == 4 else exchange_tiles)(*args)
    shared = pl.pallas_call(
        share_kernel,
        out_shape=jax.ShapeDtypeStruct((grids, levels) + panel.shape, jnp.float32),
        in_specs=[VMEM],
        out_specs=VMEM,
        scratch_shapes=[
            pltpu.SemaphoreType.DMA((12,)),
            pltpu.SemaphoreType.DMA((12,)),
            pltpu.SemaphoreType.DMA,
        ],
        compiler_params=pltpu.CompilerParams(collective_id=1, has_side_effects=True),
        name="share",
    )(panel)
    result = pl.pallas_call(
        schur_kernel,
        out_shape=jax.ShapeDtypeStruct(assembled.shape, jnp.float32),
        in_specs=[VMEM, VMEM, VMEM],
        out_specs=VMEM,
        compiler_params=pltpu.CompilerParams(vmem_limit_bytes=32 * 1024 * 1024),
        name="schur",
    )(assembled, panel, shared)
    return result.reshape(parent_front.shape)


def solution(mesh):
    return jax.shard_map(
        per_device,
        mesh=mesh,
        in_specs=(
            P("front", None, "grid", "lvl", None, None),
            P("front"),
            P("lvl", "front", "grid", None),
            P("lvl", "front", "grid", None),
            P("lvl", "front", "grid", None, None),
            P("lvl", "front", "grid", None),
            P(),
            P("front", None, "grid", "lvl", None, None),
        ),
        out_specs=P("front", None, "grid", "lvl", None, None),
        check_vma=False,
    )
```

```python
import functools

import jax
import jax.numpy as jnp
from jax import lax
from jax.experimental import pallas as pl
from jax.experimental.pallas import tpu as pltpu
from jax.sharding import PartitionSpec as P

BLOCK = 256
NB = 32
SUB = 8
HIGHEST = lax.Precision.HIGHEST
NT = (((1,), (1,)), ((), ()))
TN = (((0,), (0,)), ((), ()))


def eliminate(work, inverse):
    n = BLOCK
    row_ids = lax.broadcasted_iota(jnp.int32, (NB, 1), 0)

    def step(kb, carry):
        rows = work[:NB, :]
        for sub in range(NB // SUB):
            first = sub * SUB
            cols = [
                jnp.broadcast_to(rows[:, first + i : first + i + 1], (NB, 128))
                for i in range(SUB)
            ]
            for i in range(SUB):
                j = first + i
                inv = lax.rsqrt(cols[i][j : j + 1, :])
                below = jnp.where(row_ids > j, cols[i] * inv, 0.0)
                for m in range(i + 1, SUB):
                    cols[m] = cols[m] - below * (cols[m][j : j + 1, :] * inv)
                inv_wide = jnp.concatenate([inv] * (2 * n // 128), axis=1)
                below_wide = jnp.concatenate([below] * (2 * n // 128), axis=1)
                urow = rows[j : j + 1, :] * inv_wide
                rows = jnp.where(row_ids == j, urow, rows - below_wide * urow)
        at = pl.ds(pl.multiple_of(kb * NB, NB), NB)
        inverse[at, :] = pltpu.roll(rows, kb * NB + n, 1)[:, :n]
        update = lax.dot_general(
            rows[:, :n], rows, TN, precision=HIGHEST, preferred_element_type=jnp.float32
        )
        rest = work[NB:, :] - update[NB:, :]
        work[: n - NB, :] = pltpu.roll(rest, 2 * n - NB, 1)
        return carry

    lax.fori_loop(0, n // NB, step, 0)


def assemble_kernel(
    meta_own, meta_pivot, gathered, parent, raw_pivot, acc, pivot, tiles, pivot_tiles
):
    fronts, grids, levels, local, half, depth = gathered.shape
    blocks = grids * local
    me_g, me_l = lax.axis_index("grid"), lax.axis_index("lvl")
    most = meta_own.shape[2]

    def gram(step, carry):
        f, g = step // grids, step % grids
        right = gathered[f, g].reshape(levels * local * half, depth)
        left = jnp.concatenate(
            [
                gathered[f, me_g, me_l].reshape(local * half, depth),
                gathered[f, 0].reshape(levels * local * half, depth),
            ],
            axis=0,
        )
        prod = lax.dot_general(left, right, NT, preferred_element_type=jnp.float32)
        prod = (-prod).astype(jnp.bfloat16)
        for r in range(local):
            for s in range(local):
                at = f * (local * blocks) + r * blocks + s * grids + g
                for m in range(levels):
                    lane = (m * local + s) * half
                    tiles[at, :, m * half : (m + 1) * half] = prod[
                        r * half : (r + 1) * half, lane : lane + half
                    ]
                    for lv in range(levels):
                        row = (local + lv * local + r) * half
                        pivot_tiles[lv, at, :, m * half : (m + 1) * half] = prod[
                            row : row + half, lane : lane + half
                        ]
        return carry

    lax.fori_loop(0, fronts * grids, gram, 0)
    whole = [raw_pivot[lv] for lv in range(levels)]
    for lv in range(levels):
        rows = slice(lv * half, (lv + 1) * half)
        pivot[rows, :] = whole[lv]
        for f in range(fronts):

            def add_pivot(k, carry, lv=lv, f=f, rows=rows):
                @pl.when(meta_pivot[lv, f, 2, k] == 0)
                def _():
                    at = (f * local + meta_pivot[lv, f, 0, k]) * blocks + meta_pivot[lv, f, 1, k]
                    pivot[rows, :] = pivot[rows, :] + pivot_tiles[lv, at].astype(jnp.float32)

                return carry

            lax.fori_loop(0, meta_pivot[lv, f, 3, 0], add_pivot, 0)
    acc[...] = parent[...]
    width_blocks = parent.shape[2] // BLOCK
    for f in range(fronts):

        def add_own(k, carry, f=f):
            at = (f * local + meta_own[f, 0, k]) * blocks + meta_own[f, 1, k]
            place = meta_own[f, 2, k]
            r = place // width_blocks
            lanes = pl.ds(pl.multiple_of(place % width_blocks * BLOCK, BLOCK), BLOCK)
            acc[r, :, lanes] = acc[r, :, lanes] + tiles[at].astype(jnp.float32)
            return carry

        lax.fori_loop(0, meta_own[f, 3, 0], add_own, 0)


def schur_kernel(acc, inverse, shared, out):
    local, half, width = acc.shape
    grids, levels = shared.shape[0], shared.shape[1]

    def panel_of(column):
        return lax.dot_general(
            column, inverse[...], NT, precision=HIGHEST, preferred_element_type=jnp.float32
        )

    rows = panel_of(acc[:, :, :BLOCK].reshape(local * half, BLOCK))
    out[:, :, :BLOCK] = rows.reshape(local, half, BLOCK)
    for g in range(grids):
        piece = panel_of(shared[g].reshape(levels * local * half, BLOCK))
        prod = lax.dot_general(
            rows, piece, NT, precision=HIGHEST, preferred_element_type=jnp.float32
        ).reshape(local, half, levels * local * half)
        for lv in range(levels):
            for s in range(local):
                if s == 0 and g == 0:
                    continue
                lane = (s * grids + g) * BLOCK + lv * half
                at = (lv * local + s) * half
                out[:, :, lane : lane + half] = (
                    acc[:, :, lane : lane + half] - prod[:, :, at : at + half]
                )


class Sends:
    def __init__(self, send_sems, recv_sems):
        self.send_sems, self.recv_sems, self.used, self.started = send_sems, recv_sems, 0, []

    def make(self, src, dst, device):
        copy = pltpu.make_async_remote_copy(
            src_ref=src,
            dst_ref=dst,
            send_sem=self.send_sems.at[self.used],
            recv_sem=self.recv_sems.at[self.used],
            device_id=device,
            device_id_type=pl.DeviceIdType.MESH,
        )
        self.used += 1
        return copy

    def start(self, src, dst, device):
        copy = self.make(src, dst, device)
        copy.start()
        self.started.append(copy)
        return copy

    def finish(self):
        for copy in self.started:
            copy.wait_send()


def greet(devices):
    barrier = pltpu.get_barrier_semaphore()
    for device in devices:
        pl.semaphore_signal(barrier, inc=1, device_id=device, device_id_type=pl.DeviceIdType.MESH)
    pl.semaphore_wait(barrier, len(devices))


def plane_peers():
    level, grid = lax.axis_index("lvl"), lax.axis_index("grid")
    across = grid + 1 - 2 * (grid % 2)
    along = (grid + 2) % 4
    return level, grid, across, along


def gather_kernel(
    own, meta, first, out, meta_own, meta_pivot, raw, send_sems, recv_sems, local_sems
):
    level, grid, across, along = plane_peers()
    corner = (across + 2) % 4
    front = lax.axis_index("front")
    order = [front + 1 - 2 * (front % 2), (front + 2) % 4, 3 - front]

    def at_front(f):
        return {"front": f}

    x_peer, y_peer, core = {"grid": across}, {"grid": along}, {"lvl": 1 - level}
    greet([at_front(f) for f in order] + [x_peer, y_peer, {"grid": corner}, core])
    sends = Sends(send_sems, recv_sems)
    locals_ = [
        pltpu.make_async_copy(own, out.at[front, grid, level], local_sems.at[0]),
        pltpu.make_async_copy(meta.at[front], meta_own.at[front], local_sems.at[1]),
    ]
    for copy in locals_:
        copy.start()
    meta_z = [sends.start(meta.at[f], meta_own.at[front], at_front(f)) for f in order]
    panel_z = [sends.start(own, out.at[front, grid, level], at_front(f)) for f in order]
    to_x, to_y, to_core = [], [], []

    def spread(f, source):
        place = out.at[f, grid, level]
        to_x.append(sends.start(source, place, x_peer))
        to_y.append(sends.start(source, place, y_peer))
        to_core.append(sends.start(source, place, core))

    spread(front, own)
    planes = [front] + order

    raw_at = raw.at[level]
    piv_at = meta_pivot.at[level]
    raw_copies = [sends.make(first, raw_at, {"grid": g}) for g in (1, 2, 3)]
    piv_copies = [sends.make(meta_own, piv_at, {"grid": g}) for g in (1, 2, 3)]
    raw_local = pltpu.make_async_copy(first, raw_at, local_sems.at[2])
    piv_local = pltpu.make_async_copy(meta_own, piv_at, local_sems.at[3])

    locals_[1].wait()
    for copy in meta_z:
        copy.wait_recv()

    @pl.when(grid == 0)
    def _():
        piv_local.start()
        raw_local.start()
        for copy in piv_copies + raw_copies:
            copy.start()
        piv_local.wait()
        raw_local.wait()

    for g in (1, 2, 3):

        @pl.when(grid == g)
        def _(g=g):
            piv_copies[g - 1].wait_recv()
            raw_copies[g - 1].wait_recv()

    small = [sends.start(piv_at, piv_at, core), sends.start(raw_at, raw_at, core)]
    corners = []

    def forward(k):
        f = planes[k]
        to_x[k].wait_recv()
        place = out.at[f, across, level]
        half = out.at[f, across, level, 0]
        corners.append(sends.start(half, half, y_peer))
        to_core.append(sends.start(place, place, core))
        to_y[k].wait_recv()
        place = out.at[f, along, level]
        half = out.at[f, along, level, 1]
        corners.append(sends.start(half, half, x_peer))
        to_core.append(sends.start(place, place, core))

    def corner_in(k):
        place = out.at[planes[k], corner, level]
        corners[2 * k].wait_recv()
        corners[2 * k + 1].wait_recv()
        to_core.append(sends.start(place, place, core))

    for k in (1, 2, 3):
        panel_z[k - 1].wait_recv()
        place = out.at[planes[k], grid, level]
        spread(planes[k], place)
        forward(k - 1)
        if k > 1:
            corner_in(k - 2)
    forward(3)
    corner_in(2)
    corner_in(3)
    locals_[0].wait()
    for copy in to_core + small:
        copy.wait_recv()
    sends.finish()

    @pl.when(grid == 0)
    def _():
        for copy in piv_copies + raw_copies:
            copy.wait_send()


def share_kernel(own, pivot, out, inverse, work, send_sems, recv_sems, local_sem):
    level, grid, across, along = plane_peers()
    corner = (across + 2) % 4
    x_peer, y_peer, core = {"grid": across}, {"grid": along}, {"lvl": 1 - level}
    greet([x_peer, y_peer, core])
    sends = Sends(send_sems, recv_sems)
    local = out.shape[2]
    mine = pltpu.make_async_copy(own, out.at[grid, level], local_sem)
    to_x = [None] * local
    to_y = [None] * local
    to_core = []
    for r in range(local):
        place = out.at[grid, level, r]
        to_x[r] = sends.start(own.at[r], place, x_peer)
        place = out.at[grid, level, local - 1 - r]
        to_y[local - 1 - r] = sends.start(own.at[local - 1 - r], place, y_peer)
    to_core.append(sends.start(own, out.at[grid, level], core))
    mine.start()
    whole = pivot[...]
    work[:, :BLOCK] = 0.5 * (whole + whole.T)
    work[:, BLOCK:] = (
        lax.broadcasted_iota(jnp.int32, (BLOCK, BLOCK), 0)
        == lax.broadcasted_iota(jnp.int32, (BLOCK, BLOCK), 1)
    ).astype(jnp.float32)
    eliminate(work, inverse)
    to_x[0].wait_recv()
    half = out.at[across, level, 0]
    corner_y = sends.start(half, half, y_peer)
    to_y[1].wait_recv()
    half = out.at[along, level, 1]
    corner_x = sends.start(half, half, x_peer)
    for r in range(1, local):
        to_x[r].wait_recv()
    place = out.at[across, level]
    to_core.append(sends.start(place, place, core))
    to_y[0].wait_recv()
    place = out.at[along, level]
    to_core.append(sends.start(place, place, core))
    corner_y.wait_recv()
    half = out.at[corner, level, 0]
    to_core.append(sends.start(half, half, core))
    corner_x.wait_recv()
    half = out.at[corner, level, 1]
    to_core.append(sends.start(half, half, core))
    mine.wait()
    for copy in to_core:
        copy.wait_recv()
    sends.finish()


VMEM = pl.BlockSpec(memory_space=pltpu.VMEM)
ANY = pl.BlockSpec(memory_space=pl.ANY)
SMEM = pl.BlockSpec(memory_space=pltpu.SMEM)


def owner_of(parents, parent_owner):
    ids = jnp.arange(parent_owner.shape[0], dtype=jnp.int32)
    return jnp.sum(jnp.where(parents[..., None] == ids, parent_owner, 0), axis=-1)


def gather_all(
    child_panel, child_blocks, tile_rows, tile_cols, tile_parent, tile_place, parent_owner, parent_front
):
    levels, grids, fronts = lax.axis_size("lvl"), lax.axis_size("grid"), lax.axis_size("front")
    me_l, me_g, me_f = lax.axis_index("lvl"), lax.axis_index("grid"), lax.axis_index("front")
    local, half, depth = child_panel.shape[1], child_panel.shape[4], child_panel.shape[5]
    rows_in = child_panel.reshape(1, local, half, depth)
    slots = tile_rows.shape[3]
    blocks = local * grids
    row = tile_rows.reshape(slots)
    col = tile_cols.reshape(slots)
    live = (row * grids + me_g < child_blocks[0]) & (col < child_blocks[0])
    to = owner_of(tile_parent.reshape(slots), parent_owner)
    most = 2 * slots // fronts
    sent = (to[None, :] == jnp.arange(fronts, dtype=jnp.int32)[:, None]) & live[None, :]
    before = jnp.arange(slots)[:, None] < jnp.arange(slots)[None, :]
    rank = jnp.sum(jnp.where(before[None] & sent[:, :, None], 1, 0), axis=1)
    match = (rank[:, None, :] == jnp.arange(most, dtype=jnp.int32)[None, :, None]) & sent[:, None, :]
    fields = jnp.stack([row, col, tile_place.reshape(slots), jnp.zeros_like(row)])
    meta = jnp.sum(jnp.where(match[:, None], fields[None, :, None, :], 0), axis=3)
    total = jnp.sum(sent.astype(jnp.int32), axis=1)[:, None, None]
    meta = jnp.where(jnp.arange(4)[None, :, None] == 3, total, meta)
    gathered, meta_own, meta_pivot, raw_pivot = pl.pallas_call(
        gather_kernel,
        out_shape=(
            jax.ShapeDtypeStruct((fronts, grids, levels, local, half, depth), jnp.bfloat16),
            jax.ShapeDtypeStruct((fronts, 4, most), jnp.int32),
            jax.ShapeDtypeStruct((levels, fronts, 4, most), jnp.int32),
            jax.ShapeDtypeStruct((levels, half, BLOCK), jnp.float32),
        ),
        in_specs=[VMEM, VMEM, VMEM],
        out_specs=(VMEM, VMEM, VMEM, VMEM),
        scratch_shapes=[
            pltpu.SemaphoreType.DMA((64,)),
            pltpu.SemaphoreType.DMA((64,)),
            pltpu.SemaphoreType.DMA((4,)),
        ],
        compiler_params=pltpu.CompilerParams(
            collective_id=0, has_side_effects=True, vmem_limit_bytes=24 * 1024 * 1024
        ),
        name="gather",
    )(rows_in[0], meta, parent_front[0, 0, 0, 0, :, :BLOCK])
    parent = parent_front.reshape(parent_front.shape[1], half, parent_front.shape[5])
    return pl.pallas_call(
        assemble_kernel,
        out_shape=(
            jax.ShapeDtypeStruct(parent.shape, jnp.float32),
            jax.ShapeDtypeStruct((BLOCK, BLOCK), jnp.float32),
        ),
        in_specs=[SMEM, SMEM, VMEM, VMEM, VMEM],
        out_specs=(VMEM, VMEM),
        scratch_shapes=[
            pltpu.VMEM((fronts * local * blocks, half, BLOCK), jnp.bfloat16),
            pltpu.VMEM((levels, fronts * local * blocks, half, BLOCK), jnp.bfloat16),
        ],
        compiler_params=pltpu.CompilerParams(vmem_limit_bytes=30 * 1024 * 1024),
        name="assemble",
    )(meta_own, meta_pivot, gathered, parent, raw_pivot)


def exchange_tiles(
    child_panel, child_blocks, tile_rows, tile_cols, tile_parent, tile_place, parent_owner, parent_front
):
    levels, grids, fronts = lax.axis_size("lvl"), lax.axis_size("grid"), lax.axis_size("front")
    grid_index = lax.axis_index("grid")
    local, half, depth = child_panel.shape[1], child_panel.shape[4], child_panel.shape[5]
    parent_local, width = parent_front.shape[1], parent_front.shape[5]
    slots = tile_rows.shape[3]
    blocks = width // BLOCK
    capacity = 2 * slots // fronts
    own = child_panel.reshape(local * half, depth)
    view = lax.all_gather(
        own.reshape(1, local, half, depth), ("grid", "lvl"), axis=0, tiled=True
    ).reshape(grids, levels, local, half, depth)
    gram = jnp.einsum("ik,glsjk->isglj", own, view, preferred_element_type=jnp.float32)
    gram = (-gram).astype(jnp.bfloat16).reshape(local, half, local * grids, BLOCK)
    gram = gram.transpose(0, 2, 1, 3).reshape(local * local * grids, half, BLOCK)
    row, col = tile_rows.reshape(slots), tile_cols.reshape(slots)
    live = (row * grids + grid_index < child_blocks[0]) & (col < child_blocks[0])
    ids = jnp.arange(fronts, dtype=jnp.int32)
    owners = owner_of(tile_parent.reshape(slots), parent_owner)
    one_hot = (owners[:, None] == ids[None, :]).astype(jnp.int32)
    rank = jnp.sum((jnp.cumsum(one_hot, axis=0) - 1) * one_hot, axis=1)
    index = owners * capacity + rank
    matches = index[None, :] == jnp.arange(fronts * capacity, dtype=jnp.int32)[:, None]
    filled = jnp.any(matches & live[None, :], axis=1)
    source = jnp.sum(jnp.where(matches, (row * local * grids + col)[None, :], 0), axis=1)
    place = jnp.sum(jnp.where(matches, tile_place.reshape(slots)[None, :], 0), axis=1)
    outgoing = jnp.where(filled[:, None, None], gram[source], jnp.zeros((), jnp.bfloat16))
    positions = jnp.where(filled, place, -1)
    incoming = lax.all_to_all(outgoing, "front", split_axis=0, concat_axis=0, tiled=True)
    landed = lax.all_to_all(positions, "front", split_axis=0, concat_axis=0, tiled=True)
    spots = parent_local * blocks
    selector = (landed[:, None] == jnp.arange(spots, dtype=jnp.int32)[None, :]).astype(jnp.bfloat16)
    contrib = jnp.einsum("sk,sij->kij", selector, incoming, preferred_element_type=jnp.float32)
    contrib = contrib.reshape(parent_local, blocks, half, BLOCK).transpose(0, 2, 1, 3)
    assembled = parent_front.reshape(parent_local, half, width) + contrib.reshape(
        parent_local, half, width
    )
    raw = lax.all_gather(assembled[0, :, :BLOCK][None], ("grid", "lvl"), axis=0, tiled=True)
    raw = raw[:levels].reshape(levels * half, BLOCK)
    return assembled, raw


def per_device(*args):
    levels, grids, fronts = lax.axis_size("lvl"), lax.axis_size("grid"), lax.axis_size("front")
    parent_front = args[-1]
    assembled, pivot = (gather_all if fronts == 4 else exchange_tiles)(*args)
    column = assembled[:, :, :BLOCK]
    shared, inverse = pl.pallas_call(
        share_kernel,
        out_shape=(
            jax.ShapeDtypeStruct((grids, levels) + column.shape, jnp.float32),
            jax.ShapeDtypeStruct((BLOCK, BLOCK), jnp.float32),
        ),
        in_specs=[VMEM, VMEM],
        out_specs=(VMEM, VMEM),
        scratch_shapes=[
            pltpu.VMEM((BLOCK, 2 * BLOCK), jnp.float32),
            pltpu.SemaphoreType.DMA((12,)),
            pltpu.SemaphoreType.DMA((12,)),
            pltpu.SemaphoreType.DMA,
        ],
        compiler_params=pltpu.CompilerParams(
            collective_id=1, has_side_effects=True, vmem_limit_bytes=16 * 1024 * 1024
        ),
        name="share",
    )(column, pivot)
    result = pl.pallas_call(
        schur_kernel,
        out_shape=jax.ShapeDtypeStruct(assembled.shape, jnp.float32),
        in_specs=[VMEM, VMEM, VMEM],
        out_specs=VMEM,
        compiler_params=pltpu.CompilerParams(vmem_limit_bytes=20 * 1024 * 1024),
        name="schur",
    )(assembled, inverse, shared)
    return result.reshape(parent_front.shape)


def solution(mesh):
    return jax.shard_map(
        per_device,
        mesh=mesh,
        in_specs=(
            P("front", None, "grid", "lvl", None, None),
            P("front"),
            P("lvl", "front", "grid", None),
            P("lvl", "front", "grid", None),
            P("lvl", "front", "grid", None, None),
            P("lvl", "front", "grid", None),
            P(),
            P("front", None, "grid", "lvl", None, None),
        ),
        out_specs=P("front", None, "grid", "lvl", None, None),
        check_vma=False,
    )
```

```python
import functools

import jax
import jax.numpy as jnp
from jax import lax
from jax.experimental import pallas as pl
from jax.experimental.pallas import tpu as pltpu
from jax.sharding import PartitionSpec as P

BLOCK = 256
NB = 32
SUB = 8
HIGHEST = lax.Precision.HIGHEST
NT = (((1,), (1,)), ((), ()))
TN = (((0,), (0,)), ((), ()))


def eliminate(work, inverse, begin, end):
    n = BLOCK
    row_ids = lax.broadcasted_iota(jnp.int32, (NB, 1), 0)

    def step(kb, carry):
        rows = work[:NB, :]
        for sub in range(NB // SUB):
            first = sub * SUB
            cols = [
                jnp.broadcast_to(rows[:, first + i : first + i + 1], (NB, 128))
                for i in range(SUB)
            ]
            for i in range(SUB):
                j = first + i
                inv = lax.rsqrt(cols[i][j : j + 1, :])
                below = jnp.where(row_ids > j, cols[i] * inv, 0.0)
                for m in range(i + 1, SUB):
                    cols[m] = cols[m] - below * (cols[m][j : j + 1, :] * inv)
                inv_wide = jnp.concatenate([inv] * (2 * n // 128), axis=1)
                below_wide = jnp.concatenate([below] * (2 * n // 128), axis=1)
                urow = rows[j : j + 1, :] * inv_wide
                rows = jnp.where(row_ids == j, urow, rows - below_wide * urow)
        at = pl.ds(pl.multiple_of(kb * NB, NB), NB)
        inverse[at, :] = pltpu.roll(rows, kb * NB + n, 1)[:, :n]
        update = lax.dot_general(
            rows[:, :n], rows, TN, precision=HIGHEST, preferred_element_type=jnp.float32
        )
        rest = work[NB:, :] - update[NB:, :]
        work[: n - NB, :] = pltpu.roll(rest, 2 * n - NB, 1)
        return carry

    lax.fori_loop(begin, end, step, 0)


def assemble_kernel(
    meta_own, meta_pivot, gathered, parent, raw_pivot, acc, pivot, tiles, pivot_tiles
):
    fronts, grids, levels, local, half, depth = gathered.shape
    blocks = grids * local
    me_g, me_l = lax.axis_index("grid"), lax.axis_index("lvl")
    most = meta_own.shape[2]

    def gram(step, carry):
        f, g = step // grids, step % grids
        right = gathered[f, g].reshape(levels * local * half, depth)
        left = jnp.concatenate(
            [
                gathered[f, me_g, me_l].reshape(local * half, depth),
                gathered[f, 0].reshape(levels * local * half, depth),
            ],
            axis=0,
        )
        prod = lax.dot_general(left, right, NT, preferred_element_type=jnp.float32)
        prod = (-prod).astype(jnp.bfloat16)
        for r in range(local):
            for s in range(local):
                at = f * (local * blocks) + r * blocks + s * grids + g
                for m in range(levels):
                    lane = (m * local + s) * half
                    tiles[at, :, m * half : (m + 1) * half] = prod[
                        r * half : (r + 1) * half, lane : lane + half
                    ]
                    for lv in range(levels):
                        row = (local + lv * local + r) * half
                        pivot_tiles[lv, at, :, m * half : (m + 1) * half] = prod[
                            row : row + half, lane : lane + half
                        ]
        return carry

    lax.fori_loop(0, fronts * grids, gram, 0)
    whole = [raw_pivot[lv] for lv in range(levels)]
    for lv in range(levels):
        rows = slice(lv * half, (lv + 1) * half)
        pivot[rows, :] = whole[lv]
        for f in range(fronts):

            def add_pivot(k, carry, lv=lv, f=f, rows=rows):
                @pl.when(meta_pivot[lv, f, 2, k] == 0)
                def _():
                    at = (f * local + meta_pivot[lv, f, 0, k]) * blocks + meta_pivot[lv, f, 1, k]
                    pivot[rows, :] = pivot[rows, :] + pivot_tiles[lv, at].astype(jnp.float32)

                return carry

            lax.fori_loop(0, meta_pivot[lv, f, 3, 0], add_pivot, 0)
    acc[...] = parent[...]
    width_blocks = parent.shape[2] // BLOCK
    for f in range(fronts):

        def add_own(k, carry, f=f):
            at = (f * local + meta_own[f, 0, k]) * blocks + meta_own[f, 1, k]
            place = meta_own[f, 2, k]
            r = place // width_blocks
            lanes = pl.ds(pl.multiple_of(place % width_blocks * BLOCK, BLOCK), BLOCK)
            acc[r, :, lanes] = acc[r, :, lanes] + tiles[at].astype(jnp.float32)
            return carry

        lax.fori_loop(0, meta_own[f, 3, 0], add_own, 0)


def schur_kernel(acc, inverse, shared, out):
    local, half, width = acc.shape
    grids, levels = shared.shape[0], shared.shape[1]

    def panel_of(column):
        return lax.dot_general(
            column, inverse[...], NT, precision=HIGHEST, preferred_element_type=jnp.float32
        )

    rows = panel_of(acc[:, :, :BLOCK].reshape(local * half, BLOCK))
    out[:, :, :BLOCK] = rows.reshape(local, half, BLOCK)
    for g in range(grids):
        piece = panel_of(shared[g].reshape(levels * local * half, BLOCK))
        prod = lax.dot_general(
            rows, piece, NT, precision=HIGHEST, preferred_element_type=jnp.float32
        ).reshape(local, half, levels * local * half)
        for lv in range(levels):
            for s in range(local):
                if s == 0 and g == 0:
                    continue
                lane = (s * grids + g) * BLOCK + lv * half
                at = (lv * local + s) * half
                out[:, :, lane : lane + half] = (
                    acc[:, :, lane : lane + half] - prod[:, :, at : at + half]
                )


class Sends:
    def __init__(self, send_sems, recv_sems):
        self.send_sems, self.recv_sems, self.used, self.started = send_sems, recv_sems, 0, []

    def make(self, src, dst, device):
        copy = pltpu.make_async_remote_copy(
            src_ref=src,
            dst_ref=dst,
            send_sem=self.send_sems.at[self.used],
            recv_sem=self.recv_sems.at[self.used],
            device_id=device,
            device_id_type=pl.DeviceIdType.MESH,
        )
        self.used += 1
        return copy

    def start(self, src, dst, device):
        copy = self.make(src, dst, device)
        copy.start()
        self.started.append(copy)
        return copy

    def finish(self):
        for copy in self.started:
            copy.wait_send()


def greet(devices):
    barrier = pltpu.get_barrier_semaphore()
    for device in devices:
        pl.semaphore_signal(barrier, inc=1, device_id=device, device_id_type=pl.DeviceIdType.MESH)
    pl.semaphore_wait(barrier, len(devices))


def plane_peers():
    level, grid = lax.axis_index("lvl"), lax.axis_index("grid")
    across = grid + 1 - 2 * (grid % 2)
    along = (grid + 2) % 4
    return level, grid, across, along


def gather_kernel(
    own, meta, first, out, meta_own, meta_pivot, raw, send_sems, recv_sems, local_sems
):
    level, grid, across, along = plane_peers()
    corner = (across + 2) % 4
    front = lax.axis_index("front")
    order = [front + 1 - 2 * (front % 2), (front + 2) % 4, 3 - front]

    def at_front(f):
        return {"front": f}

    x_peer, y_peer, core = {"grid": across}, {"grid": along}, {"lvl": 1 - level}
    greet([at_front(f) for f in order] + [x_peer, y_peer, {"grid": corner}, core])
    sends = Sends(send_sems, recv_sems)
    locals_ = [
        pltpu.make_async_copy(own, out.at[front, grid, level], local_sems.at[0]),
        pltpu.make_async_copy(meta.at[front], meta_own.at[front], local_sems.at[1]),
    ]
    for copy in locals_:
        copy.start()
    meta_z = [sends.start(meta.at[f], meta_own.at[front], at_front(f)) for f in order]
    panel_z = [sends.make(own, out.at[front, grid, level], at_front(f)) for f in order]
    panel_z[0].start()
    to_x, to_y, to_core = [], [], []

    def spread(f, source):
        place = out.at[f, grid, level]
        to_x.append(sends.start(source, place, x_peer))
        to_y.append(sends.start(source, place, y_peer))
        to_core.append(sends.start(source, place, core))

    spread(front, own)
    planes = [front] + order

    raw_at = raw.at[level]
    piv_at = meta_pivot.at[level]
    raw_copies = [sends.make(first, raw_at, {"grid": g}) for g in (1, 2, 3)]
    piv_copies = [sends.make(meta_own, piv_at, {"grid": g}) for g in (1, 2, 3)]
    raw_local = pltpu.make_async_copy(first, raw_at, local_sems.at[2])
    piv_local = pltpu.make_async_copy(meta_own, piv_at, local_sems.at[3])

    locals_[1].wait()
    for copy in meta_z:
        copy.wait_recv()

    @pl.when(grid == 0)
    def _():
        piv_local.start()
        raw_local.start()
        for copy in piv_copies + raw_copies:
            copy.start()
        piv_local.wait()
        raw_local.wait()

    for g in (1, 2, 3):

        @pl.when(grid == g)
        def _(g=g):
            piv_copies[g - 1].wait_recv()
            raw_copies[g - 1].wait_recv()

    small = [sends.start(piv_at, piv_at, core), sends.start(raw_at, raw_at, core)]
    corners = []

    def forward(k):
        f = planes[k]
        to_x[k].wait_recv()
        place = out.at[f, across, level]
        half = out.at[f, across, level, 0]
        corners.append(sends.start(half, half, y_peer))
        to_core.append(sends.start(place, place, core))
        to_y[k].wait_recv()
        place = out.at[f, along, level]
        half = out.at[f, along, level, 1]
        corners.append(sends.start(half, half, x_peer))
        to_core.append(sends.start(place, place, core))

    def corner_in(k):
        place = out.at[planes[k], corner, level]
        corners[2 * k].wait_recv()
        corners[2 * k + 1].wait_recv()
        to_core.append(sends.start(place, place, core))

    for k in (1, 2, 3):
        panel_z[k - 1].wait()
        if k < 3:
            panel_z[k].start()
        place = out.at[planes[k], grid, level]
        spread(planes[k], place)
        forward(k - 1)
        if k > 1:
            corner_in(k - 2)
    forward(3)
    corner_in(2)
    corner_in(3)
    locals_[0].wait()
    for copy in to_core + small:
        copy.wait_recv()
    sends.finish()

    @pl.when(grid == 0)
    def _():
        for copy in piv_copies + raw_copies:
            copy.wait_send()


def share_kernel(own, pivot, out, inverse, work, send_sems, recv_sems, local_sem):
    level, grid, across, along = plane_peers()
    corner = (across + 2) % 4
    x_peer, y_peer, core = {"grid": across}, {"grid": along}, {"lvl": 1 - level}
    greet([x_peer, y_peer, core])
    sends = Sends(send_sems, recv_sems)
    local = out.shape[2]
    mine = pltpu.make_async_copy(own, out.at[grid, level], local_sem)
    to_x = [None] * local
    to_y = [None] * local
    to_core = []
    for r in range(local):
        place = out.at[grid, level, r]
        to_x[r] = sends.start(own.at[r], place, x_peer)
        place = out.at[grid, level, local - 1 - r]
        to_y[local - 1 - r] = sends.start(own.at[local - 1 - r], place, y_peer)
    to_core.append(sends.start(own, out.at[grid, level], core))
    mine.start()
    whole = pivot[...]
    work[:, :BLOCK] = 0.5 * (whole + whole.T)
    work[:, BLOCK:] = (
        lax.broadcasted_iota(jnp.int32, (BLOCK, BLOCK), 0)
        == lax.broadcasted_iota(jnp.int32, (BLOCK, BLOCK), 1)
    ).astype(jnp.float32)
    eliminate(work, inverse, 0, 5)
    to_x[0].wait_recv()
    half = out.at[across, level, 0]
    corner_y = sends.start(half, half, y_peer)
    to_y[1].wait_recv()
    half = out.at[along, level, 1]
    corner_x = sends.start(half, half, x_peer)
    for r in range(1, local):
        to_x[r].wait_recv()
    place = out.at[across, level]
    to_core.append(sends.start(place, place, core))
    to_y[0].wait_recv()
    place = out.at[along, level]
    to_core.append(sends.start(place, place, core))
    eliminate(work, inverse, 5, BLOCK // NB)
    corner_y.wait_recv()
    half = out.at[corner, level, 0]
    to_core.append(sends.start(half, half, core))
    corner_x.wait_recv()
    half = out.at[corner, level, 1]
    to_core.append(sends.start(half, half, core))
    mine.wait()
    for copy in to_core:
        copy.wait_recv()
    sends.finish()


VMEM = pl.BlockSpec(memory_space=pltpu.VMEM)
ANY = pl.BlockSpec(memory_space=pl.ANY)
SMEM = pl.BlockSpec(memory_space=pltpu.SMEM)


def owner_of(parents, parent_owner):
    ids = jnp.arange(parent_owner.shape[0], dtype=jnp.int32)
    return jnp.sum(jnp.where(parents[..., None] == ids, parent_owner, 0), axis=-1)


def gather_all(
    child_panel, child_blocks, tile_rows, tile_cols, tile_parent, tile_place, parent_owner, parent_front
):
    levels, grids, fronts = lax.axis_size("lvl"), lax.axis_size("grid"), lax.axis_size("front")
    me_l, me_g, me_f = lax.axis_index("lvl"), lax.axis_index("grid"), lax.axis_index("front")
    local, half, depth = child_panel.shape[1], child_panel.shape[4], child_panel.shape[5]
    rows_in = child_panel.reshape(1, local, half, depth)
    slots = tile_rows.shape[3]
    blocks = local * grids
    row = tile_rows.reshape(slots)
    col = tile_cols.reshape(slots)
    live = (row * grids + me_g < child_blocks[0]) & (col < child_blocks[0])
    to = owner_of(tile_parent.reshape(slots), parent_owner)
    most = 2 * slots // fronts
    sent = (to[None, :] == jnp.arange(fronts, dtype=jnp.int32)[:, None]) & live[None, :]
    before = jnp.arange(slots)[:, None] < jnp.arange(slots)[None, :]
    rank = jnp.sum(jnp.where(before[None] & sent[:, :, None], 1, 0), axis=1)
    match = (rank[:, None, :] == jnp.arange(most, dtype=jnp.int32)[None, :, None]) & sent[:, None, :]
    fields = jnp.stack([row, col, tile_place.reshape(slots), jnp.zeros_like(row)])
    meta = jnp.sum(jnp.where(match[:, None], fields[None, :, None, :], 0), axis=3)
    total = jnp.sum(sent.astype(jnp.int32), axis=1)[:, None, None]
    meta = jnp.where(jnp.arange(4)[None, :, None] == 3, total, meta)
    gathered, meta_own, meta_pivot, raw_pivot = pl.pallas_call(
        gather_kernel,
        out_shape=(
            jax.ShapeDtypeStruct((fronts, grids, levels, local, half, depth), jnp.bfloat16),
            jax.ShapeDtypeStruct((fronts, 4, most), jnp.int32),
            jax.ShapeDtypeStruct((levels, fronts, 4, most), jnp.int32),
            jax.ShapeDtypeStruct((levels, half, BLOCK), jnp.float32),
        ),
        in_specs=[VMEM, VMEM, VMEM],
        out_specs=(VMEM, VMEM, VMEM, VMEM),
        scratch_shapes=[
            pltpu.SemaphoreType.DMA((64,)),
            pltpu.SemaphoreType.DMA((64,)),
            pltpu.SemaphoreType.DMA((4,)),
        ],
        compiler_params=pltpu.CompilerParams(
            collective_id=0, has_side_effects=True, vmem_limit_bytes=24 * 1024 * 1024
        ),
        name="gather",
    )(rows_in[0], meta, parent_front[0, 0, 0, 0, :, :BLOCK])
    parent = parent_front.reshape(parent_front.shape[1], half, parent_front.shape[5])
    return pl.pallas_call(
        assemble_kernel,
        out_shape=(
            jax.ShapeDtypeStruct(parent.shape, jnp.float32),
            jax.ShapeDtypeStruct((BLOCK, BLOCK), jnp.float32),
        ),
        in_specs=[SMEM, SMEM, VMEM, VMEM, VMEM],
        out_specs=(VMEM, VMEM),
        scratch_shapes=[
            pltpu.VMEM((fronts * local * blocks, half, BLOCK), jnp.bfloat16),
            pltpu.VMEM((levels, fronts * local * blocks, half, BLOCK), jnp.bfloat16),
        ],
        compiler_params=pltpu.CompilerParams(vmem_limit_bytes=30 * 1024 * 1024),
        name="assemble",
    )(meta_own, meta_pivot, gathered, parent, raw_pivot)


def exchange_tiles(
    child_panel, child_blocks, tile_rows, tile_cols, tile_parent, tile_place, parent_owner, parent_front
):
    levels, grids, fronts = lax.axis_size("lvl"), lax.axis_size("grid"), lax.axis_size("front")
    grid_index = lax.axis_index("grid")
    local, half, depth = child_panel.shape[1], child_panel.shape[4], child_panel.shape[5]
    parent_local, width = parent_front.shape[1], parent_front.shape[5]
    slots = tile_rows.shape[3]
    blocks = width // BLOCK
    capacity = 2 * slots // fronts
    own = child_panel.reshape(local * half, depth)
    view = lax.all_gather(
        own.reshape(1, local, half, depth), ("grid", "lvl"), axis=0, tiled=True
    ).reshape(grids, levels, local, half, depth)
    gram = jnp.einsum("ik,glsjk->isglj", own, view, preferred_element_type=jnp.float32)
    gram = (-gram).astype(jnp.bfloat16).reshape(local, half, local * grids, BLOCK)
    gram = gram.transpose(0, 2, 1, 3).reshape(local * local * grids, half, BLOCK)
    row, col = tile_rows.reshape(slots), tile_cols.reshape(slots)
    live = (row * grids + grid_index < child_blocks[0]) & (col < child_blocks[0])
    ids = jnp.arange(fronts, dtype=jnp.int32)
    owners = owner_of(tile_parent.reshape(slots), parent_owner)
    one_hot = (owners[:, None] == ids[None, :]).astype(jnp.int32)
    rank = jnp.sum((jnp.cumsum(one_hot, axis=0) - 1) * one_hot, axis=1)
    index = owners * capacity + rank
    matches = index[None, :] == jnp.arange(fronts * capacity, dtype=jnp.int32)[:, None]
    filled = jnp.any(matches & live[None, :], axis=1)
    source = jnp.sum(jnp.where(matches, (row * local * grids + col)[None, :], 0), axis=1)
    place = jnp.sum(jnp.where(matches, tile_place.reshape(slots)[None, :], 0), axis=1)
    outgoing = jnp.where(filled[:, None, None], gram[source], jnp.zeros((), jnp.bfloat16))
    positions = jnp.where(filled, place, -1)
    incoming = lax.all_to_all(outgoing, "front", split_axis=0, concat_axis=0, tiled=True)
    landed = lax.all_to_all(positions, "front", split_axis=0, concat_axis=0, tiled=True)
    spots = parent_local * blocks
    selector = (landed[:, None] == jnp.arange(spots, dtype=jnp.int32)[None, :]).astype(jnp.bfloat16)
    contrib = jnp.einsum("sk,sij->kij", selector, incoming, preferred_element_type=jnp.float32)
    contrib = contrib.reshape(parent_local, blocks, half, BLOCK).transpose(0, 2, 1, 3)
    assembled = parent_front.reshape(parent_local, half, width) + contrib.reshape(
        parent_local, half, width
    )
    raw = lax.all_gather(assembled[0, :, :BLOCK][None], ("grid", "lvl"), axis=0, tiled=True)
    raw = raw[:levels].reshape(levels * half, BLOCK)
    return assembled, raw


def per_device(*args):
    levels, grids, fronts = lax.axis_size("lvl"), lax.axis_size("grid"), lax.axis_size("front")
    parent_front = args[-1]
    assembled, pivot = (gather_all if fronts == 4 else exchange_tiles)(*args)
    column = assembled[:, :, :BLOCK]
    shared, inverse = pl.pallas_call(
        share_kernel,
        out_shape=(
            jax.ShapeDtypeStruct((grids, levels) + column.shape, jnp.float32),
            jax.ShapeDtypeStruct((BLOCK, BLOCK), jnp.float32),
        ),
        in_specs=[VMEM, VMEM],
        out_specs=(VMEM, VMEM),
        scratch_shapes=[
            pltpu.VMEM((BLOCK, 2 * BLOCK), jnp.float32),
            pltpu.SemaphoreType.DMA((12,)),
            pltpu.SemaphoreType.DMA((12,)),
            pltpu.SemaphoreType.DMA,
        ],
        compiler_params=pltpu.CompilerParams(
            collective_id=1, has_side_effects=True, vmem_limit_bytes=16 * 1024 * 1024
        ),
        name="share",
    )(column, pivot)
    result = pl.pallas_call(
        schur_kernel,
        out_shape=jax.ShapeDtypeStruct(assembled.shape, jnp.float32),
        in_specs=[VMEM, VMEM, VMEM],
        out_specs=VMEM,
        compiler_params=pltpu.CompilerParams(vmem_limit_bytes=20 * 1024 * 1024),
        name="schur",
    )(assembled, inverse, shared)
    return result.reshape(parent_front.shape)


def solution(mesh):
    return jax.shard_map(
        per_device,
        mesh=mesh,
        in_specs=(
            P("front", None, "grid", "lvl", None, None),
            P("front"),
            P("lvl", "front", "grid", None),
            P("lvl", "front", "grid", None),
            P("lvl", "front", "grid", None, None),
            P("lvl", "front", "grid", None),
            P(),
            P("front", None, "grid", "lvl", None, None),
        ),
        out_specs=P("front", None, "grid", "lvl", None, None),
        check_vma=False,
    )
```

```python
import functools

import jax
import jax.numpy as jnp
from jax import lax
from jax.experimental import pallas as pl
from jax.experimental.pallas import tpu as pltpu
from jax.sharding import PartitionSpec as P

BLOCK = 256
NB = 32
SUB = 8
HIGHEST = lax.Precision.HIGHEST
NT = (((1,), (1,)), ((), ()))
TN = (((0,), (0,)), ((), ()))


def eliminate(work, inverse, begin, end):
    n = BLOCK
    row_ids = lax.broadcasted_iota(jnp.int32, (NB, 1), 0)

    def step(kb, carry):
        rows = work[:NB, :]
        for sub in range(NB // SUB):
            first = sub * SUB
            cols = [
                jnp.broadcast_to(rows[:, first + i : first + i + 1], (NB, 128))
                for i in range(SUB)
            ]
            for i in range(SUB):
                j = first + i
                inv = lax.rsqrt(cols[i][j : j + 1, :])
                below = jnp.where(row_ids > j, cols[i] * inv, 0.0)
                for m in range(i + 1, SUB):
                    cols[m] = cols[m] - below * (cols[m][j : j + 1, :] * inv)
                inv_wide = jnp.concatenate([inv] * (2 * n // 128), axis=1)
                below_wide = jnp.concatenate([below] * (2 * n // 128), axis=1)
                urow = rows[j : j + 1, :] * inv_wide
                rows = jnp.where(row_ids == j, urow, rows - below_wide * urow)
        at = pl.ds(pl.multiple_of(kb * NB, NB), NB)
        inverse[at, :] = pltpu.roll(rows, kb * NB + n, 1)[:, :n]
        update = lax.dot_general(
            rows[:, :n], rows, TN, precision=HIGHEST, preferred_element_type=jnp.float32
        )
        rest = work[NB:, :] - update[NB:, :]
        work[: n - NB, :] = pltpu.roll(rest, 2 * n - NB, 1)
        return carry

    lax.fori_loop(begin, end, step, 0)


def gram_of_child(f, gathered, tiles, pivot_tiles):
    fronts, grids, levels, local, half, depth = gathered.shape
    blocks = grids * local
    me_g, me_l = lax.axis_index("grid"), lax.axis_index("lvl")

    def gram(g, carry):
        right = gathered[f, g].reshape(levels * local * half, depth)
        left = jnp.concatenate(
            [
                gathered[f, me_g, me_l].reshape(local * half, depth),
                gathered[f, 0].reshape(levels * local * half, depth),
            ],
            axis=0,
        )
        prod = lax.dot_general(left, right, NT, preferred_element_type=jnp.float32)
        prod = (-prod).astype(jnp.bfloat16)
        for r in range(local):
            for s in range(local):
                at = f * (local * blocks) + r * blocks + s * grids + g
                for m in range(levels):
                    lane = (m * local + s) * half
                    tiles[at, :, m * half : (m + 1) * half] = prod[
                        r * half : (r + 1) * half, lane : lane + half
                    ]
                    for lv in range(levels):
                        row = (local + lv * local + r) * half
                        pivot_tiles[lv, at, :, m * half : (m + 1) * half] = prod[
                            row : row + half, lane : lane + half
                        ]
        return carry

    lax.fori_loop(0, grids, gram, 0)


def assemble_kernel(
    meta_own, meta_pivot, tiles, pivot_tiles, parent, raw_pivot, acc, pivot
):
    fronts, local = meta_own.shape[0], parent.shape[0]
    levels, half = pivot_tiles.shape[0], parent.shape[1]
    blocks = tiles.shape[0] // (fronts * local)
    whole = [raw_pivot[lv] for lv in range(levels)]
    for lv in range(levels):
        rows = slice(lv * half, (lv + 1) * half)
        pivot[rows, :] = whole[lv]
        for f in range(fronts):

            def add_pivot(k, carry, lv=lv, f=f, rows=rows):
                @pl.when(meta_pivot[lv, f, 2, k] == 0)
                def _():
                    at = (f * local + meta_pivot[lv, f, 0, k]) * blocks + meta_pivot[lv, f, 1, k]
                    pivot[rows, :] = pivot[rows, :] + pivot_tiles[lv, at].astype(jnp.float32)

                return carry

            lax.fori_loop(0, meta_pivot[lv, f, 3, 0], add_pivot, 0)
    acc[...] = parent[...]
    width_blocks = parent.shape[2] // BLOCK
    for f in range(fronts):

        def add_own(k, carry, f=f):
            at = (f * local + meta_own[f, 0, k]) * blocks + meta_own[f, 1, k]
            place = meta_own[f, 2, k]
            r = place // width_blocks
            lanes = pl.ds(pl.multiple_of(place % width_blocks * BLOCK, BLOCK), BLOCK)
            acc[r, :, lanes] = acc[r, :, lanes] + tiles[at].astype(jnp.float32)
            return carry

        lax.fori_loop(0, meta_own[f, 3, 0], add_own, 0)


def schur_kernel(acc, inverse, shared, out):
    local, half, width = acc.shape
    grids, levels = shared.shape[0], shared.shape[1]

    def panel_of(column):
        return lax.dot_general(
            column, inverse[...], NT, precision=HIGHEST, preferred_element_type=jnp.float32
        )

    rows = panel_of(acc[:, :, :BLOCK].reshape(local * half, BLOCK))
    out[:, :, :BLOCK] = rows.reshape(local, half, BLOCK)
    for g in range(grids):
        piece = panel_of(shared[g].reshape(levels * local * half, BLOCK))
        prod = lax.dot_general(
            rows, piece, NT, precision=HIGHEST, preferred_element_type=jnp.float32
        ).reshape(local, half, levels * local * half)
        for lv in range(levels):
            for s in range(local):
                if s == 0 and g == 0:
                    continue
                lane = (s * grids + g) * BLOCK + lv * half
                at = (lv * local + s) * half
                out[:, :, lane : lane + half] = (
                    acc[:, :, lane : lane + half] - prod[:, :, at : at + half]
                )


class Sends:
    def __init__(self, send_sems, recv_sems):
        self.send_sems, self.recv_sems, self.used, self.started = send_sems, recv_sems, 0, []

    def make(self, src, dst, device):
        copy = pltpu.make_async_remote_copy(
            src_ref=src,
            dst_ref=dst,
            send_sem=self.send_sems.at[self.used],
            recv_sem=self.recv_sems.at[self.used],
            device_id=device,
            device_id_type=pl.DeviceIdType.MESH,
        )
        self.used += 1
        return copy

    def start(self, src, dst, device):
        copy = self.make(src, dst, device)
        copy.start()
        self.started.append(copy)
        return copy

    def finish(self):
        for copy in self.started:
            copy.wait_send()


def greet(devices):
    barrier = pltpu.get_barrier_semaphore()
    for device in devices:
        pl.semaphore_signal(barrier, inc=1, device_id=device, device_id_type=pl.DeviceIdType.MESH)
    pl.semaphore_wait(barrier, len(devices))


def plane_peers():
    level, grid = lax.axis_index("lvl"), lax.axis_index("grid")
    across = grid + 1 - 2 * (grid % 2)
    along = (grid + 2) % 4
    return level, grid, across, along


def gather_kernel(
    own, meta, first, tiles, pivot_tiles, meta_own, meta_pivot, raw,
    out, send_sems, recv_sems, local_sems,
):
    level, grid, across, along = plane_peers()
    corner = (across + 2) % 4
    front = lax.axis_index("front")
    order = [front + 1 - 2 * (front % 2), (front + 2) % 4, 3 - front]

    def at_front(f):
        return {"front": f}

    x_peer, y_peer, core = {"grid": across}, {"grid": along}, {"lvl": 1 - level}
    greet([at_front(f) for f in order] + [x_peer, y_peer, {"grid": corner}, core])
    sends = Sends(send_sems, recv_sems)
    locals_ = [
        pltpu.make_async_copy(own, out.at[front, grid, level], local_sems.at[0]),
        pltpu.make_async_copy(meta.at[front], meta_own.at[front], local_sems.at[1]),
    ]
    for copy in locals_:
        copy.start()
    meta_z = [sends.start(meta.at[f], meta_own.at[front], at_front(f)) for f in order]
    panel_z = [sends.start(own, out.at[front, grid, level], at_front(f)) for f in order]
    to_x, to_y = [], []
    landing = [[] for _ in range(4)]

    def spread(k, f, source):
        place = out.at[f, grid, level]
        to_x.append(sends.start(source, place, x_peer))
        to_y.append(sends.start(source, place, y_peer))
        landing[k].append(sends.start(source, place, core))

    spread(0, front, own)
    planes = [front] + order

    raw_at = raw.at[level]
    piv_at = meta_pivot.at[level]
    raw_copies = [sends.make(first, raw_at, {"grid": g}) for g in (1, 2, 3)]
    piv_copies = [sends.make(meta_own, piv_at, {"grid": g}) for g in (1, 2, 3)]
    raw_local = pltpu.make_async_copy(first, raw_at, local_sems.at[2])
    piv_local = pltpu.make_async_copy(meta_own, piv_at, local_sems.at[3])

    corners = []

    def forward(k):
        f = planes[k]
        to_x[k].wait_recv()
        place = out.at[f, across, level]
        half = out.at[f, across, level, 0]
        corners.append(sends.start(half, half, y_peer))
        landing[k].append(sends.start(place, place, core))
        to_y[k].wait_recv()
        place = out.at[f, along, level]
        half = out.at[f, along, level, 1]
        corners.append(sends.start(half, half, x_peer))
        landing[k].append(sends.start(place, place, core))

    def corner_in(k):
        place = out.at[planes[k], corner, level]
        corners[2 * k].wait_recv()
        corners[2 * k + 1].wait_recv()
        landing[k].append(sends.start(place, place, core))

    def multiply(k):
        if k == 0:
            locals_[0].wait()
        for copy in landing[k]:
            copy.wait_recv()
        gram_of_child(planes[k], out, tiles, pivot_tiles)

    def small_out():
        locals_[1].wait()
        for copy in meta_z:
            copy.wait_recv()

        @pl.when(grid == 0)
        def _():
            piv_local.start()
            raw_local.start()
            for copy in piv_copies + raw_copies:
                copy.start()
            piv_local.wait()
            raw_local.wait()

    for k in (1, 2, 3):
        panel_z[k - 1].wait_recv()
        place = out.at[planes[k], grid, level]
        spread(k, planes[k], place)
        forward(k - 1)
        if k == 1:
            small_out()
        else:
            corner_in(k - 2)
            multiply(k - 2)
    forward(3)
    corner_in(2)
    multiply(2)
    corner_in(3)
    for g in (1, 2, 3):

        @pl.when(grid == g)
        def _(g=g):
            piv_copies[g - 1].wait_recv()
            raw_copies[g - 1].wait_recv()

    small = [sends.start(piv_at, piv_at, core), sends.start(raw_at, raw_at, core)]
    multiply(3)
    for copy in small:
        copy.wait_recv()
    sends.finish()

    @pl.when(grid == 0)
    def _():
        for copy in piv_copies + raw_copies:
            copy.wait_send()


def share_kernel(own, pivot, out, inverse, work, send_sems, recv_sems, local_sem):
    level, grid, across, along = plane_peers()
    corner = (across + 2) % 4
    x_peer, y_peer, core = {"grid": across}, {"grid": along}, {"lvl": 1 - level}
    greet([x_peer, y_peer, core])
    sends = Sends(send_sems, recv_sems)
    local = out.shape[2]
    mine = pltpu.make_async_copy(own, out.at[grid, level], local_sem)
    to_x = [None] * local
    to_y = [None] * local
    to_core = []
    for r in range(local):
        place = out.at[grid, level, r]
        to_x[r] = sends.start(own.at[r], place, x_peer)
        place = out.at[grid, level, local - 1 - r]
        to_y[local - 1 - r] = sends.start(own.at[local - 1 - r], place, y_peer)
    to_core.append(sends.start(own, out.at[grid, level], core))
    mine.start()
    whole = pivot[...]
    work[:, :BLOCK] = 0.5 * (whole + whole.T)
    work[:, BLOCK:] = (
        lax.broadcasted_iota(jnp.int32, (BLOCK, BLOCK), 0)
        == lax.broadcasted_iota(jnp.int32, (BLOCK, BLOCK), 1)
    ).astype(jnp.float32)
    eliminate(work, inverse, 0, 5)
    to_x[0].wait_recv()
    half = out.at[across, level, 0]
    corner_y = sends.start(half, half, y_peer)
    to_y[1].wait_recv()
    half = out.at[along, level, 1]
    corner_x = sends.start(half, half, x_peer)
    for r in range(1, local):
        to_x[r].wait_recv()
    place = out.at[across, level]
    to_core.append(sends.start(place, place, core))
    to_y[0].wait_recv()
    place = out.at[along, level]
    to_core.append(sends.start(place, place, core))
    eliminate(work, inverse, 5, BLOCK // NB)
    corner_y.wait_recv()
    half = out.at[corner, level, 0]
    to_core.append(sends.start(half, half, core))
    corner_x.wait_recv()
    half = out.at[corner, level, 1]
    to_core.append(sends.start(half, half, core))
    mine.wait()
    for copy in to_core:
        copy.wait_recv()
    sends.finish()


VMEM = pl.BlockSpec(memory_space=pltpu.VMEM)
ANY = pl.BlockSpec(memory_space=pl.ANY)
SMEM = pl.BlockSpec(memory_space=pltpu.SMEM)


def owner_of(parents, parent_owner):
    ids = jnp.arange(parent_owner.shape[0], dtype=jnp.int32)
    return jnp.sum(jnp.where(parents[..., None] == ids, parent_owner, 0), axis=-1)


def gather_all(
    child_panel, child_blocks, tile_rows, tile_cols, tile_parent, tile_place, parent_owner, parent_front
):
    levels, grids, fronts = lax.axis_size("lvl"), lax.axis_size("grid"), lax.axis_size("front")
    me_l, me_g, me_f = lax.axis_index("lvl"), lax.axis_index("grid"), lax.axis_index("front")
    local, half, depth = child_panel.shape[1], child_panel.shape[4], child_panel.shape[5]
    rows_in = child_panel.reshape(1, local, half, depth)
    slots = tile_rows.shape[3]
    blocks = local * grids
    row = tile_rows.reshape(slots)
    col = tile_cols.reshape(slots)
    live = (row * grids + me_g < child_blocks[0]) & (col < child_blocks[0])
    to = owner_of(tile_parent.reshape(slots), parent_owner)
    most = 2 * slots // fronts
    sent = (to[None, :] == jnp.arange(fronts, dtype=jnp.int32)[:, None]) & live[None, :]
    before = jnp.arange(slots)[:, None] < jnp.arange(slots)[None, :]
    rank = jnp.sum(jnp.where(before[None] & sent[:, :, None], 1, 0), axis=1)
    match = (rank[:, None, :] == jnp.arange(most, dtype=jnp.int32)[None, :, None]) & sent[:, None, :]
    fields = jnp.stack([row, col, tile_place.reshape(slots), jnp.zeros_like(row)])
    meta = jnp.sum(jnp.where(match[:, None], fields[None, :, None, :], 0), axis=3)
    total = jnp.sum(sent.astype(jnp.int32), axis=1)[:, None, None]
    meta = jnp.where(jnp.arange(4)[None, :, None] == 3, total, meta)
    tiles, pivot_tiles, meta_own, meta_pivot, raw_pivot = pl.pallas_call(
        gather_kernel,
        out_shape=(
            jax.ShapeDtypeStruct((fronts * local * blocks, half, BLOCK), jnp.bfloat16),
            jax.ShapeDtypeStruct((levels, fronts * local * blocks, half, BLOCK), jnp.bfloat16),
            jax.ShapeDtypeStruct((fronts, 4, most), jnp.int32),
            jax.ShapeDtypeStruct((levels, fronts, 4, most), jnp.int32),
            jax.ShapeDtypeStruct((levels, half, BLOCK), jnp.float32),
        ),
        in_specs=[VMEM, VMEM, VMEM],
        out_specs=(VMEM, VMEM, VMEM, VMEM, VMEM),
        scratch_shapes=[
            pltpu.VMEM((fronts, grids, levels, local, half, depth), jnp.bfloat16),
            pltpu.SemaphoreType.DMA((64,)),
            pltpu.SemaphoreType.DMA((64,)),
            pltpu.SemaphoreType.DMA((4,)),
        ],
        compiler_params=pltpu.CompilerParams(
            collective_id=0, has_side_effects=True, vmem_limit_bytes=32 * 1024 * 1024
        ),
        name="gather",
    )(rows_in[0], meta, parent_front[0, 0, 0, 0, :, :BLOCK])
    parent = parent_front.reshape(parent_front.shape[1], half, parent_front.shape[5])
    return pl.pallas_call(
        assemble_kernel,
        out_shape=(
            jax.ShapeDtypeStruct(parent.shape, jnp.float32),
            jax.ShapeDtypeStruct((BLOCK, BLOCK), jnp.float32),
        ),
        in_specs=[SMEM, SMEM, VMEM, VMEM, VMEM, VMEM],
        out_specs=(VMEM, VMEM),
        compiler_params=pltpu.CompilerParams(vmem_limit_bytes=24 * 1024 * 1024),
        name="assemble",
    )(meta_own, meta_pivot, tiles, pivot_tiles, parent, raw_pivot)


def exchange_tiles(
    child_panel, child_blocks, tile_rows, tile_cols, tile_parent, tile_place, parent_owner, parent_front
):
    levels, grids, fronts = lax.axis_size("lvl"), lax.axis_size("grid"), lax.axis_size("front")
    grid_index = lax.axis_index("grid")
    local, half, depth = child_panel.shape[1], child_panel.shape[4], child_panel.shape[5]
    parent_local, width = parent_front.shape[1], parent_front.shape[5]
    slots = tile_rows.shape[3]
    blocks = width // BLOCK
    capacity = 2 * slots // fronts
    own = child_panel.reshape(local * half, depth)
    view = lax.all_gather(
        own.reshape(1, local, half, depth), ("grid", "lvl"), axis=0, tiled=True
    ).reshape(grids, levels, local, half, depth)
    gram = jnp.einsum("ik,glsjk->isglj", own, view, preferred_element_type=jnp.float32)
    gram = (-gram).astype(jnp.bfloat16).reshape(local, half, local * grids, BLOCK)
    gram = gram.transpose(0, 2, 1, 3).reshape(local * local * grids, half, BLOCK)
    row, col = tile_rows.reshape(slots), tile_cols.reshape(slots)
    live = (row * grids + grid_index < child_blocks[0]) & (col < child_blocks[0])
    ids = jnp.arange(fronts, dtype=jnp.int32)
    owners = owner_of(tile_parent.reshape(slots), parent_owner)
    one_hot = (owners[:, None] == ids[None, :]).astype(jnp.int32)
    rank = jnp.sum((jnp.cumsum(one_hot, axis=0) - 1) * one_hot, axis=1)
    index = owners * capacity + rank
    matches = index[None, :] == jnp.arange(fronts * capacity, dtype=jnp.int32)[:, None]
    filled = jnp.any(matches & live[None, :], axis=1)
    source = jnp.sum(jnp.where(matches, (row * local * grids + col)[None, :], 0), axis=1)
    place = jnp.sum(jnp.where(matches, tile_place.reshape(slots)[None, :], 0), axis=1)
    outgoing = jnp.where(filled[:, None, None], gram[source], jnp.zeros((), jnp.bfloat16))
    positions = jnp.where(filled, place, -1)
    incoming = lax.all_to_all(outgoing, "front", split_axis=0, concat_axis=0, tiled=True)
    landed = lax.all_to_all(positions, "front", split_axis=0, concat_axis=0, tiled=True)
    spots = parent_local * blocks
    selector = (landed[:, None] == jnp.arange(spots, dtype=jnp.int32)[None, :]).astype(jnp.bfloat16)
    contrib = jnp.einsum("sk,sij->kij", selector, incoming, preferred_element_type=jnp.float32)
    contrib = contrib.reshape(parent_local, blocks, half, BLOCK).transpose(0, 2, 1, 3)
    assembled = parent_front.reshape(parent_local, half, width) + contrib.reshape(
        parent_local, half, width
    )
    raw = lax.all_gather(assembled[0, :, :BLOCK][None], ("grid", "lvl"), axis=0, tiled=True)
    raw = raw[:levels].reshape(levels * half, BLOCK)
    return assembled, raw


def per_device(*args):
    levels, grids, fronts = lax.axis_size("lvl"), lax.axis_size("grid"), lax.axis_size("front")
    parent_front = args[-1]
    assembled, pivot = (gather_all if fronts == 4 else exchange_tiles)(*args)
    column = assembled[:, :, :BLOCK]
    shared, inverse = pl.pallas_call(
        share_kernel,
        out_shape=(
            jax.ShapeDtypeStruct((grids, levels) + column.shape, jnp.float32),
            jax.ShapeDtypeStruct((BLOCK, BLOCK), jnp.float32),
        ),
        in_specs=[VMEM, VMEM],
        out_specs=(VMEM, VMEM),
        scratch_shapes=[
            pltpu.VMEM((BLOCK, 2 * BLOCK), jnp.float32),
            pltpu.SemaphoreType.DMA((12,)),
            pltpu.SemaphoreType.DMA((12,)),
            pltpu.SemaphoreType.DMA,
        ],
        compiler_params=pltpu.CompilerParams(
            collective_id=1, has_side_effects=True, vmem_limit_bytes=16 * 1024 * 1024
        ),
        name="share",
    )(column, pivot)
    result = pl.pallas_call(
        schur_kernel,
        out_shape=jax.ShapeDtypeStruct(assembled.shape, jnp.float32),
        in_specs=[VMEM, VMEM, VMEM],
        out_specs=VMEM,
        compiler_params=pltpu.CompilerParams(vmem_limit_bytes=20 * 1024 * 1024),
        name="schur",
    )(assembled, inverse, shared)
    return result.reshape(parent_front.shape)


def solution(mesh):
    return jax.shard_map(
        per_device,
        mesh=mesh,
        in_specs=(
            P("front", None, "grid", "lvl", None, None),
            P("front"),
            P("lvl", "front", "grid", None),
            P("lvl", "front", "grid", None),
            P("lvl", "front", "grid", None, None),
            P("lvl", "front", "grid", None),
            P(),
            P("front", None, "grid", "lvl", None, None),
        ),
        out_specs=P("front", None, "grid", "lvl", None, None),
        check_vma=False,
    )
```

```python
import functools

import jax
import jax.numpy as jnp
from jax import lax
from jax.experimental import pallas as pl
from jax.experimental.pallas import tpu as pltpu
from jax.sharding import PartitionSpec as P

BLOCK = 256
NB = 32
SUB = 8
HIGHEST = lax.Precision.HIGHEST
NT = (((1,), (1,)), ((), ()))
TN = (((0,), (0,)), ((), ()))


def eliminate(work, inverse, begin, end):
    n = BLOCK
    row_ids = lax.broadcasted_iota(jnp.int32, (NB, 1), 0)

    def step(kb, carry):
        rows = work[:NB, :]
        for sub in range(NB // SUB):
            first = sub * SUB
            cols = [
                jnp.broadcast_to(rows[:, first + i : first + i + 1], (NB, 128))
                for i in range(SUB)
            ]
            for i in range(SUB):
                j = first + i
                inv = lax.rsqrt(cols[i][j : j + 1, :])
                below = jnp.where(row_ids > j, cols[i] * inv, 0.0)
                for m in range(i + 1, SUB):
                    cols[m] = cols[m] - below * (cols[m][j : j + 1, :] * inv)
                inv_wide = jnp.concatenate([inv] * (2 * n // 128), axis=1)
                below_wide = jnp.concatenate([below] * (2 * n // 128), axis=1)
                urow = rows[j : j + 1, :] * inv_wide
                rows = jnp.where(row_ids == j, urow, rows - below_wide * urow)
        at = pl.ds(pl.multiple_of(kb * NB, NB), NB)
        inverse[at, :] = pltpu.roll(rows, kb * NB + n, 1)[:, :n]
        update = lax.dot_general(
            rows[:, :n], rows, TN, precision=HIGHEST, preferred_element_type=jnp.float32
        )
        rest = work[NB:, :] - update[NB:, :]
        work[: n - NB, :] = pltpu.roll(rest, 2 * n - NB, 1)
        return carry

    lax.fori_loop(begin, end, step, 0)


def gram_of_child(f, gathered, tiles, pivot_tiles):
    fronts, grids, levels, local, half, depth = gathered.shape
    blocks = grids * local
    me_g, me_l = lax.axis_index("grid"), lax.axis_index("lvl")

    def gram(g, carry):
        right = gathered[f, g].reshape(levels * local * half, depth)
        left = jnp.concatenate(
            [
                gathered[f, me_g, me_l].reshape(local * half, depth),
                gathered[f, 0].reshape(levels * local * half, depth),
            ],
            axis=0,
        )
        prod = lax.dot_general(left, right, NT, preferred_element_type=jnp.float32)
        prod = (-prod).astype(jnp.bfloat16)
        for r in range(local):
            for s in range(local):
                at = f * (local * blocks) + r * blocks + s * grids + g
                for m in range(levels):
                    lane = (m * local + s) * half
                    tiles[at, :, m * half : (m + 1) * half] = prod[
                        r * half : (r + 1) * half, lane : lane + half
                    ]
                    for lv in range(levels):
                        row = (local + lv * local + r) * half
                        pivot_tiles[lv, at, :, m * half : (m + 1) * half] = prod[
                            row : row + half, lane : lane + half
                        ]
        return carry

    lax.fori_loop(0, grids, gram, 0)


def assemble_kernel(
    meta_own, meta_pivot, tiles, pivot_tiles, parent, raw_pivot, acc, pivot
):
    fronts, local = meta_own.shape[0], parent.shape[0]
    levels, half = pivot_tiles.shape[0], parent.shape[1]
    blocks = tiles.shape[0] // (fronts * local)
    whole = [raw_pivot[lv] for lv in range(levels)]
    for lv in range(levels):
        rows = slice(lv * half, (lv + 1) * half)
        pivot[rows, :] = whole[lv]
        for f in range(fronts):

            def add_pivot(k, carry, lv=lv, f=f, rows=rows):
                @pl.when(meta_pivot[lv, f, 2, k] == 0)
                def _():
                    at = (f * local + meta_pivot[lv, f, 0, k]) * blocks + meta_pivot[lv, f, 1, k]
                    pivot[rows, :] = pivot[rows, :] + pivot_tiles[lv, at].astype(jnp.float32)

                return carry

            lax.fori_loop(0, meta_pivot[lv, f, 3, 0], add_pivot, 0)
    acc[...] = parent[...]
    width_blocks = parent.shape[2] // BLOCK
    for f in range(fronts):

        def add_own(k, carry, f=f):
            at = (f * local + meta_own[f, 0, k]) * blocks + meta_own[f, 1, k]
            place = meta_own[f, 2, k]
            r = place // width_blocks
            lanes = pl.ds(pl.multiple_of(place % width_blocks * BLOCK, BLOCK), BLOCK)
            acc[r, :, lanes] = acc[r, :, lanes] + tiles[at].astype(jnp.float32)
            return carry

        lax.fori_loop(0, meta_own[f, 3, 0], add_own, 0)


def schur_kernel(acc, inverse, shared, out):
    local, half, width = acc.shape
    grids, levels = shared.shape[0], shared.shape[1]

    def panel_of(column):
        return lax.dot_general(
            column, inverse[...], NT, precision=HIGHEST, preferred_element_type=jnp.float32
        )

    rows = panel_of(acc[:, :, :BLOCK].reshape(local * half, BLOCK))
    out[:, :, :BLOCK] = rows.reshape(local, half, BLOCK)
    for g in range(grids):
        piece = panel_of(shared[g].reshape(levels * local * half, BLOCK))
        prod = lax.dot_general(
            rows, piece, NT, precision=HIGHEST, preferred_element_type=jnp.float32
        ).reshape(local, half, levels * local * half)
        for lv in range(levels):
            for s in range(local):
                if s == 0 and g == 0:
                    continue
                lane = (s * grids + g) * BLOCK + lv * half
                at = (lv * local + s) * half
                out[:, :, lane : lane + half] = (
                    acc[:, :, lane : lane + half] - prod[:, :, at : at + half]
                )


class Sends:
    def __init__(self, send_sems, recv_sems):
        self.send_sems, self.recv_sems, self.used, self.started = send_sems, recv_sems, 0, []

    def make(self, src, dst, device):
        copy = pltpu.make_async_remote_copy(
            src_ref=src,
            dst_ref=dst,
            send_sem=self.send_sems.at[self.used],
            recv_sem=self.recv_sems.at[self.used],
            device_id=device,
            device_id_type=pl.DeviceIdType.MESH,
        )
        self.used += 1
        return copy

    def start(self, src, dst, device):
        copy = self.make(src, dst, device)
        copy.start()
        self.started.append(copy)
        return copy

    def finish(self):
        for copy in self.started:
            copy.wait_send()


def greet(devices):
    barrier = pltpu.get_barrier_semaphore()
    for device in devices:
        pl.semaphore_signal(barrier, inc=1, device_id=device, device_id_type=pl.DeviceIdType.MESH)
    pl.semaphore_wait(barrier, len(devices))


def plane_peers():
    level, grid = lax.axis_index("lvl"), lax.axis_index("grid")
    across = grid + 1 - 2 * (grid % 2)
    along = (grid + 2) % 4
    return level, grid, across, along


def gather_kernel(
    own, meta, fronts_in, tiles, pivot_tiles, meta_own, meta_pivot, raw,
    out, send_sems, recv_sems, local_sems,
):
    level, grid, across, along = plane_peers()
    corner = (across + 2) % 4
    front = lax.axis_index("front")
    order = [front + 1 - 2 * (front % 2), (front + 2) % 4, 3 - front]

    def at_front(f):
        return {"front": f}

    x_peer, y_peer, core = {"grid": across}, {"grid": along}, {"lvl": 1 - level}
    greet([at_front(f) for f in order] + [x_peer, y_peer, {"grid": corner}, core])
    sends = Sends(send_sems, recv_sems)
    locals_ = [
        pltpu.make_async_copy(own, out.at[front, grid, level], local_sems.at[0]),
        pltpu.make_async_copy(meta.at[front], meta_own.at[front], local_sems.at[1]),
    ]
    for copy in locals_:
        copy.start()
    meta_z = [sends.start(meta.at[f], meta_own.at[front], at_front(f)) for f in order]
    panel_z = [sends.start(own, out.at[front, grid, level], at_front(f)) for f in order]
    to_x, to_y = [], []
    landing = [[] for _ in range(4)]

    def spread(k, f, source):
        place = out.at[f, grid, level]
        to_x.append(sends.start(source, place, x_peer))
        to_y.append(sends.start(source, place, y_peer))
        landing[k].append(sends.start(source, place, core))

    spread(0, front, own)
    planes = [front] + order

    first = fronts_in.at[0, 0, 0, 0, :, pl.ds(0, BLOCK)]
    raw_at = raw.at[level]
    piv_at = meta_pivot.at[level]
    raw_copies = [sends.make(first, raw_at, {"grid": g}) for g in (1, 2, 3)]
    piv_copies = [sends.make(meta_own, piv_at, {"grid": g}) for g in (1, 2, 3)]
    raw_local = pltpu.make_async_copy(first, raw_at, local_sems.at[2])
    piv_local = pltpu.make_async_copy(meta_own, piv_at, local_sems.at[3])

    corners = []

    def forward(k):
        f = planes[k]
        to_x[k].wait_recv()
        place = out.at[f, across, level]
        half = out.at[f, across, level, 0]
        corners.append(sends.start(half, half, y_peer))
        landing[k].append(sends.start(place, place, core))
        to_y[k].wait_recv()
        place = out.at[f, along, level]
        half = out.at[f, along, level, 1]
        corners.append(sends.start(half, half, x_peer))
        landing[k].append(sends.start(place, place, core))

    def corner_in(k):
        place = out.at[planes[k], corner, level]
        corners[2 * k].wait_recv()
        corners[2 * k + 1].wait_recv()
        landing[k].append(sends.start(place, place, core))

    def multiply(k):
        if k == 0:
            locals_[0].wait()
        for copy in landing[k]:
            copy.wait_recv()
        gram_of_child(planes[k], out, tiles, pivot_tiles)

    def small_out():
        locals_[1].wait()
        for copy in meta_z:
            copy.wait_recv()

        @pl.when(grid == 0)
        def _():
            piv_local.start()
            raw_local.start()
            for copy in piv_copies + raw_copies:
                copy.start()
            piv_local.wait()
            raw_local.wait()

    for k in (1, 2, 3):
        panel_z[k - 1].wait_recv()
        place = out.at[planes[k], grid, level]
        spread(k, planes[k], place)
        forward(k - 1)
        if k == 1:
            small_out()
        else:
            corner_in(k - 2)
            multiply(k - 2)
    forward(3)
    corner_in(2)
    multiply(2)
    corner_in(3)
    for g in (1, 2, 3):

        @pl.when(grid == g)
        def _(g=g):
            piv_copies[g - 1].wait_recv()
            raw_copies[g - 1].wait_recv()

    small = [sends.start(piv_at, piv_at, core), sends.start(raw_at, raw_at, core)]
    multiply(3)
    for copy in small:
        copy.wait_recv()
    sends.finish()

    @pl.when(grid == 0)
    def _():
        for copy in piv_copies + raw_copies:
            copy.wait_send()


def share_kernel(own, pivot, out, inverse, work, send_sems, recv_sems, local_sem):
    level, grid, across, along = plane_peers()
    corner = (across + 2) % 4
    x_peer, y_peer, core = {"grid": across}, {"grid": along}, {"lvl": 1 - level}
    greet([x_peer, y_peer, core])
    sends = Sends(send_sems, recv_sems)
    local = out.shape[2]
    mine = pltpu.make_async_copy(own, out.at[grid, level], local_sem)
    to_x = [None] * local
    to_y = [None] * local
    to_core = []
    for r in range(local):
        place = out.at[grid, level, r]
        to_x[r] = sends.start(own.at[r], place, x_peer)
        place = out.at[grid, level, local - 1 - r]
        to_y[local - 1 - r] = sends.start(own.at[local - 1 - r], place, y_peer)
    to_core.append(sends.start(own, out.at[grid, level], core))
    mine.start()
    whole = pivot[...]
    work[:, :BLOCK] = 0.5 * (whole + whole.T)
    work[:, BLOCK:] = (
        lax.broadcasted_iota(jnp.int32, (BLOCK, BLOCK), 0)
        == lax.broadcasted_iota(jnp.int32, (BLOCK, BLOCK), 1)
    ).astype(jnp.float32)
    eliminate(work, inverse, 0, 5)
    to_x[0].wait_recv()
    half = out.at[across, level, 0]
    corner_y = sends.start(half, half, y_peer)
    to_y[1].wait_recv()
    half = out.at[along, level, 1]
    corner_x = sends.start(half, half, x_peer)
    for r in range(1, local):
        to_x[r].wait_recv()
    place = out.at[across, level]
    to_core.append(sends.start(place, place, core))
    to_y[0].wait_recv()
    place = out.at[along, level]
    to_core.append(sends.start(place, place, core))
    eliminate(work, inverse, 5, BLOCK // NB)
    corner_y.wait_recv()
    half = out.at[corner, level, 0]
    to_core.append(sends.start(half, half, core))
    corner_x.wait_recv()
    half = out.at[corner, level, 1]
    to_core.append(sends.start(half, half, core))
    mine.wait()
    for copy in to_core:
        copy.wait_recv()
    sends.finish()


VMEM = pl.BlockSpec(memory_space=pltpu.VMEM)
ANY = pl.BlockSpec(memory_space=pl.ANY)
SMEM = pl.BlockSpec(memory_space=pltpu.SMEM)


def owner_of(parents, parent_owner):
    ids = jnp.arange(parent_owner.shape[0], dtype=jnp.int32)
    return jnp.sum(jnp.where(parents[..., None] == ids, parent_owner, 0), axis=-1)


def gather_all(
    child_panel, child_blocks, tile_rows, tile_cols, tile_parent, tile_place, parent_owner, parent_front
):
    levels, grids, fronts = lax.axis_size("lvl"), lax.axis_size("grid"), lax.axis_size("front")
    me_l, me_g, me_f = lax.axis_index("lvl"), lax.axis_index("grid"), lax.axis_index("front")
    local, half, depth = child_panel.shape[1], child_panel.shape[4], child_panel.shape[5]
    rows_in = child_panel.reshape(1, local, half, depth)
    slots = tile_rows.shape[3]
    blocks = local * grids
    row = tile_rows.reshape(slots)
    col = tile_cols.reshape(slots)
    live = (row * grids + me_g < child_blocks[0]) & (col < child_blocks[0])
    to = owner_of(tile_parent.reshape(slots), parent_owner)
    most = 2 * slots // fronts
    sent = (to[None, :] == jnp.arange(fronts, dtype=jnp.int32)[:, None]) & live[None, :]
    before = jnp.arange(slots)[:, None] < jnp.arange(slots)[None, :]
    rank = jnp.sum(jnp.where(before[None] & sent[:, :, None], 1, 0), axis=1)
    match = (rank[:, None, :] == jnp.arange(most, dtype=jnp.int32)[None, :, None]) & sent[:, None, :]
    fields = jnp.stack([row, col, tile_place.reshape(slots), jnp.zeros_like(row)])
    meta = jnp.sum(jnp.where(match[:, None], fields[None, :, None, :], 0), axis=3)
    total = jnp.sum(sent.astype(jnp.int32), axis=1)[:, None, None]
    meta = jnp.where(jnp.arange(4)[None, :, None] == 3, total, meta)
    tiles, pivot_tiles, meta_own, meta_pivot, raw_pivot = pl.pallas_call(
        gather_kernel,
        out_shape=(
            jax.ShapeDtypeStruct((fronts * local * blocks, half, BLOCK), jnp.bfloat16),
            jax.ShapeDtypeStruct((levels, fronts * local * blocks, half, BLOCK), jnp.bfloat16),
            jax.ShapeDtypeStruct((fronts, 4, most), jnp.int32),
            jax.ShapeDtypeStruct((levels, fronts, 4, most), jnp.int32),
            jax.ShapeDtypeStruct((levels, half, BLOCK), jnp.float32),
        ),
        in_specs=[ANY, VMEM, ANY],
        out_specs=(VMEM, VMEM, VMEM, VMEM, VMEM),
        scratch_shapes=[
            pltpu.VMEM((fronts, grids, levels, local, half, depth), jnp.bfloat16),
            pltpu.SemaphoreType.DMA((64,)),
            pltpu.SemaphoreType.DMA((64,)),
            pltpu.SemaphoreType.DMA((4,)),
        ],
        compiler_params=pltpu.CompilerParams(
            collective_id=0, has_side_effects=True, vmem_limit_bytes=32 * 1024 * 1024
        ),
        name="gather",
    )(rows_in[0], meta, parent_front)
    parent = parent_front.reshape(parent_front.shape[1], half, parent_front.shape[5])
    return pl.pallas_call(
        assemble_kernel,
        out_shape=(
            jax.ShapeDtypeStruct(parent.shape, jnp.float32),
            jax.ShapeDtypeStruct((BLOCK, BLOCK), jnp.float32),
        ),
        in_specs=[SMEM, SMEM, VMEM, VMEM, VMEM, VMEM],
        out_specs=(VMEM, VMEM),
        compiler_params=pltpu.CompilerParams(vmem_limit_bytes=24 * 1024 * 1024),
        name="assemble",
    )(meta_own, meta_pivot, tiles, pivot_tiles, parent, raw_pivot)


def exchange_tiles(
    child_panel, child_blocks, tile_rows, tile_cols, tile_parent, tile_place, parent_owner, parent_front
):
    levels, grids, fronts = lax.axis_size("lvl"), lax.axis_size("grid"), lax.axis_size("front")
    grid_index = lax.axis_index("grid")
    local, half, depth = child_panel.shape[1], child_panel.shape[4], child_panel.shape[5]
    parent_local, width = parent_front.shape[1], parent_front.shape[5]
    slots = tile_rows.shape[3]
    blocks = width // BLOCK
    capacity = 2 * slots // fronts
    own = child_panel.reshape(local * half, depth)
    view = lax.all_gather(
        own.reshape(1, local, half, depth), ("grid", "lvl"), axis=0, tiled=True
    ).reshape(grids, levels, local, half, depth)
    gram = jnp.einsum("ik,glsjk->isglj", own, view, preferred_element_type=jnp.float32)
    gram = (-gram).astype(jnp.bfloat16).reshape(local, half, local * grids, BLOCK)
    gram = gram.transpose(0, 2, 1, 3).reshape(local * local * grids, half, BLOCK)
    row, col = tile_rows.reshape(slots), tile_cols.reshape(slots)
    live = (row * grids + grid_index < child_blocks[0]) & (col < child_blocks[0])
    ids = jnp.arange(fronts, dtype=jnp.int32)
    owners = owner_of(tile_parent.reshape(slots), parent_owner)
    one_hot = (owners[:, None] == ids[None, :]).astype(jnp.int32)
    rank = jnp.sum((jnp.cumsum(one_hot, axis=0) - 1) * one_hot, axis=1)
    index = owners * capacity + rank
    matches = index[None, :] == jnp.arange(fronts * capacity, dtype=jnp.int32)[:, None]
    filled = jnp.any(matches & live[None, :], axis=1)
    source = jnp.sum(jnp.where(matches, (row * local * grids + col)[None, :], 0), axis=1)
    place = jnp.sum(jnp.where(matches, tile_place.reshape(slots)[None, :], 0), axis=1)
    outgoing = jnp.where(filled[:, None, None], gram[source], jnp.zeros((), jnp.bfloat16))
    positions = jnp.where(filled, place, -1)
    incoming = lax.all_to_all(outgoing, "front", split_axis=0, concat_axis=0, tiled=True)
    landed = lax.all_to_all(positions, "front", split_axis=0, concat_axis=0, tiled=True)
    spots = parent_local * blocks
    selector = (landed[:, None] == jnp.arange(spots, dtype=jnp.int32)[None, :]).astype(jnp.bfloat16)
    contrib = jnp.einsum("sk,sij->kij", selector, incoming, preferred_element_type=jnp.float32)
    contrib = contrib.reshape(parent_local, blocks, half, BLOCK).transpose(0, 2, 1, 3)
    assembled = parent_front.reshape(parent_local, half, width) + contrib.reshape(
        parent_local, half, width
    )
    raw = lax.all_gather(assembled[0, :, :BLOCK][None], ("grid", "lvl"), axis=0, tiled=True)
    raw = raw[:levels].reshape(levels * half, BLOCK)
    return assembled, raw


def per_device(*args):
    levels, grids, fronts = lax.axis_size("lvl"), lax.axis_size("grid"), lax.axis_size("front")
    parent_front = args[-1]
    assembled, pivot = (gather_all if fronts == 4 else exchange_tiles)(*args)
    column = assembled[:, :, :BLOCK]
    shared, inverse = pl.pallas_call(
        share_kernel,
        out_shape=(
            jax.ShapeDtypeStruct((grids, levels) + column.shape, jnp.float32),
            jax.ShapeDtypeStruct((BLOCK, BLOCK), jnp.float32),
        ),
        in_specs=[VMEM, VMEM],
        out_specs=(VMEM, VMEM),
        scratch_shapes=[
            pltpu.VMEM((BLOCK, 2 * BLOCK), jnp.float32),
            pltpu.SemaphoreType.DMA((12,)),
            pltpu.SemaphoreType.DMA((12,)),
            pltpu.SemaphoreType.DMA,
        ],
        compiler_params=pltpu.CompilerParams(
            collective_id=1, has_side_effects=True, vmem_limit_bytes=16 * 1024 * 1024
        ),
        name="share",
    )(column, pivot)
    result = pl.pallas_call(
        schur_kernel,
        out_shape=jax.ShapeDtypeStruct(assembled.shape, jnp.float32),
        in_specs=[VMEM, VMEM, VMEM],
        out_specs=VMEM,
        compiler_params=pltpu.CompilerParams(vmem_limit_bytes=20 * 1024 * 1024),
        name="schur",
    )(assembled, inverse, shared)
    return result.reshape(parent_front.shape)


def solution(mesh):
    return jax.shard_map(
        per_device,
        mesh=mesh,
        in_specs=(
            P("front", None, "grid", "lvl", None, None),
            P("front"),
            P("lvl", "front", "grid", None),
            P("lvl", "front", "grid", None),
            P("lvl", "front", "grid", None, None),
            P("lvl", "front", "grid", None),
            P(),
            P("front", None, "grid", "lvl", None, None),
        ),
        out_specs=P("front", None, "grid", "lvl", None, None),
        check_vma=False,
    )
```
